512 devices in a mesh: row: 16 (over y, core), col: 32 (over x, z).
Axes of the slice: x: 4, y: 8, z: 8, core: 2. Of those that a mesh axis runs over, the one named last changes fastest.
Arguments:
- out_weights: bfloat16 [8192, 8192], P('row', 'col'), may hold values from -1 to 1
- in_weights: bfloat16 [8192, 8192], P('row', 'col'), may hold values from -1 to 1, as said below
- tile_list: int32 [64, 48], replicated, may hold values from 0 to 63, as said below
- tile_count: int32 [64], replicated, may hold values from 1 to 48, as said below
- owner: int32 [64], replicated, may hold values from 0 to 15, as said below
Outputs:
- transitive: float32 [8192], P('row')
- cyclic: float32 [8192], P('row')
The draws below stay inside these ranges and needn't reach their ends.
Inputs may be any that keep to these rules, and one draw needn't show every extreme that they name: in_weights is the transpose of out_weights. `tile_list`: the 48 entries of a row are distinct tile columns. Only the first tile_count[a] entries of row a of tile_list are live. `owner`: each index of row owns exactly 4 tile rows, and at most 1 of the tile rows s * 4 to (s + 1) * 4 - 1, for every s; tile row t is owned by the index (t // 4 + e) mod 16 for some e from 0 to 3.
All inputs are finite; a program needn't handle non-finite values.
Results may differ from the reference program's by a relative error of at most 0.0003.
Values may be sent and summed in bfloat16 or wider, within the bound.
No kernel may reach another device: no remote copies, remote signals or barrier semaphores. Data moves between devices by JAX's collectives and lax.ppermute only.
A program may use at most 64 MiB of HBM per device.

```python
import jax
import jax.numpy as jnp

TILE = 128
N = 8192
NT = 64
TILE_ROWS = 4
KMAX = 48


def graph_values(key):
    base_key = jax.random.fold_in(key, 11)
    key_values = jax.random.fold_in(base_key, 0)
    spread = TILE ** (-0.5)
    values = jnp.clip(jax.random.normal(key_values, (N, N), jnp.float32), -4.0, 4.0)
    return values * spread


def draw_out_weights(key, part):
    return graph_values(key).astype(jnp.bfloat16)


def draw_in_weights(key, part):
    return graph_values(key).T.astype(jnp.bfloat16)


def draw_tile_list(key, part):
    scores = jax.random.randint(jax.random.fold_in(key, 23), (NT, NT), 0, 1 << 20) * NT + jnp.arange(NT, dtype=jnp.int32)[None, :]
    return jnp.argsort(scores, axis=1, stable=True)[:, :KMAX].astype(jnp.int32)


def draw_tile_count(key, part):
    subkeys = jax.random.split(jax.random.fold_in(key, 37), 3)
    dense_row = jax.random.randint(subkeys[0], (NT,), 0, 2)
    lowest = jnp.where(dense_row == 1, KMAX // 2, KMAX // 4)
    highest = jnp.where(dense_row == 1, KMAX, KMAX // 2)
    counts = lowest + jax.random.randint(subkeys[1], (NT,), 0, 1 << 20) % (highest - lowest + 1)
    chosen = jax.random.randint(subkeys[2], (), 0, NT)
    return counts.at[chosen].set(KMAX).astype(jnp.int32)


def draw_owner(key, part):
    groups = NT // TILE_ROWS
    scores = jax.random.randint(jax.random.fold_in(key, 41), (groups, TILE_ROWS), 0, 1 << 20) * TILE_ROWS + jnp.arange(TILE_ROWS, dtype=jnp.int32)[None, :]
    offsets = jnp.argsort(scores, axis=1, stable=True).astype(jnp.int32)
    source = jnp.arange(NT, dtype=jnp.int32) // TILE_ROWS
    within = jnp.arange(NT, dtype=jnp.int32) % TILE_ROWS
    return ((source + offsets[source, within]) % groups).astype(jnp.int32)


def setup_inputs(seed: int = 0) -> dict:
    arg_keys = jax.random.split(jax.random.key(seed), 6)
    out_weights = draw_out_weights(jax.random.fold_in(arg_keys[5], 71), 0)
    in_weights = draw_in_weights(jax.random.fold_in(arg_keys[5], 71), 0)
    tile_list = draw_tile_list(jax.random.fold_in(arg_keys[5], 71), 0)
    tile_count = draw_tile_count(jax.random.fold_in(arg_keys[5], 71), 0)
    owner = draw_owner(jax.random.fold_in(arg_keys[5], 71), 0)
    return dict(out_weights=out_weights, in_weights=in_weights, tile_list=tile_list, tile_count=tile_count, owner=owner)


def tile_mask(tile_list, tile_count):
    live_slots = jnp.arange(tile_list.shape[1], dtype=jnp.int32)[None, :] < tile_count[:, None]
    matches = (tile_list[:, :, None] == jnp.arange(NT, dtype=jnp.int32)[None, None, :]) & live_slots[:, :, None]
    return jnp.any(matches, axis=1)


def spread_tiles(listed):
    return jnp.repeat(jnp.repeat(listed, TILE, axis=0), TILE, axis=1)


def reference(out_weights, in_weights, tile_list, tile_count, owner):
    listed = tile_mask(tile_list, tile_count)
    out_eff = jnp.where(spread_tiles(listed), out_weights, jnp.zeros_like(out_weights))
    in_eff = jnp.where(spread_tiles(listed.T), in_weights, jnp.zeros_like(in_weights))
    two_paths = jnp.dot(out_eff, out_eff, preferred_element_type=jnp.float32)
    trans_all = jnp.sum(out_eff.astype(jnp.float32) * two_paths, axis=1)
    cyc_all = jnp.sum(in_eff.astype(jnp.float32) * two_paths, axis=1)
    owner_order = jnp.argsort(owner, stable=True).astype(jnp.int32)
    node_order = (owner_order[:, None] * TILE + jnp.arange(TILE, dtype=jnp.int32)[None, :]).reshape(-1)
    return trans_all[node_order], cyc_all[node_order]
```

```python
import jax
import jax.numpy as jnp
import numpy as np
from jax import lax
from jax.experimental import pallas as pl
from jax.experimental.pallas import tpu as pltpu
from jax.sharding import PartitionSpec as P

TILE = 128
XS, ZS, YS, CORES = 4, 8, 8, 2
ROWS, COLS = YS * CORES, XS * ZS
VMEM = pl.BlockSpec(memory_space=pltpu.VMEM)
SMEM = pl.BlockSpec(memory_space=pltpu.SMEM)


def along_x(a, by):
    pairs = [(x * ZS + z, (x + by) % XS * ZS + z) for x in range(XS) for z in range(ZS)]
    return lax.ppermute(a, "col", pairs)


def along_z(a, by):
    pairs = [(x * ZS + z, x * ZS + (z + by) % ZS) for x in range(XS) for z in range(ZS)]
    return lax.ppermute(a, "col", pairs)


def along_row(a, by):
    return lax.ppermute(a, "row", [(i, (i + by) % ROWS) for i in range(ROWS)])


def to_lines(a):
    pairs = []
    for y in range(YS):
        for k in range(CORES):
            for x in range(XS):
                for z in range(ZS):
                    src = (y * CORES + k) * COLS + x * ZS + z
                    dst = ((y % 2 * XS + x) * CORES + k) * COLS + y // 2 * ZS + z
                    pairs.append((src, dst))
    return lax.ppermute(a, ("row", "col"), pairs)


def prologue_kernel(out_ref, in_ref, list_ref, count_ref, owner_ref, am_ref, *e_refs):
    row, col = lax.axis_index("row"), lax.axis_index("col")
    tiles = out_ref.shape[0] // TILE
    slot = lax.broadcasted_iota(jnp.int32, (1, list_ref.shape[1]), 1)

    def listed(a, b):
        hit = (list_ref[pl.ds(a, 1), :] == b) & (slot < count_ref[a])
        return jnp.max(jnp.where(hit, 1.0, 0.0), axis=1, keepdims=True)

    im_ref = e_refs[-1]
    for t in range(tiles):
        for q in range(2):
            rows, cols = pl.ds(t * TILE, TILE), pl.ds(q * TILE, TILE)
            keep = jnp.broadcast_to(listed(row * tiles + t, col * 2 + q), (TILE, TILE))
            am_ref[rows, cols] = out_ref[rows, cols] * keep.astype(out_ref.dtype)
            keep = jnp.broadcast_to(listed(col * 2 + q, row * tiles + t), (TILE, TILE))
            im_ref[rows, cols] = in_ref[rows, cols] * keep.astype(in_ref.dtype)
    for e in range(tiles):
        which = 0
        for t in range(1, tiles):
            offset = lax.rem(owner_ref[row * tiles + t] - row + ROWS, ROWS)
            which = jnp.where(offset == e, t, which)
        rows = pl.ds(pl.multiple_of(which * TILE, TILE), TILE)
        e_refs[e][0] = am_ref[rows, :]
        e_refs[e][1] = im_ref[rows, :]


def prologue(out_block, in_block, tile_list, tile_count, owner):
    rows, cols = out_block.shape
    tiles = rows // TILE
    dtype = out_block.dtype
    one = jax.ShapeDtypeStruct((2, TILE, cols), dtype)
    return pl.pallas_call(
        prologue_kernel,
        out_shape=[jax.ShapeDtypeStruct((rows, cols), dtype)] + [one] * tiles,
        in_specs=[VMEM, VMEM, VMEM, SMEM, SMEM],
        out_specs=[VMEM] * (1 + tiles),
        scratch_shapes=[pltpu.VMEM((rows, cols), dtype)],
        name="prologue",
    )(out_block, in_block, tile_list, tile_count, owner)


def census_kernel(*refs):
    a_refs, x_refs = refs[:ZS], refs[ZS : ZS + XS]
    kj_ref, res_ref = refs[ZS + XS], refs[ZS + XS + 1]
    row, col = lax.axis_index("row"), lax.axis_index("col")
    my_x, my_z = col // ZS, col % ZS
    tiles = 4
    first = jnp.minimum(row, tiles - 1)
    trans = cyc = None
    for r in range(XS):
        from_x = lax.rem(my_x + XS - r, XS)
        total = None
        for s in range(ZS):
            from_z = lax.rem(my_z + ZS - s, ZS)
            shard = (from_z // 4 * XS + from_x) * CORES + from_z % 4 // 2
            rows = pl.ds(pl.multiple_of(from_z % 2 * 256, 256), 256)
            part = jnp.dot(a_refs[s][...], kj_ref[shard, rows, :], preferred_element_type=jnp.float32)
            total = part if total is None else total + part
        t = total * x_refs[r][0].astype(jnp.float32)
        c = total * x_refs[r][1].astype(jnp.float32)
        trans = t if trans is None else trans + t
        cyc = c if cyc is None else cyc + c
    for e in range(tiles):
        place = jnp.where(e <= first, first - e, tiles + first - e)
        for which, full in ((0, trans), (1, cyc)):
            tile = full[e * TILE : (e + 1) * TILE, :]
            folded = (tile[:, :TILE] + tile[:, TILE:]).T
            res_ref[pl.ds(which * tiles + place, 1), :] = jnp.sum(folded, axis=0, keepdims=True)


def census(a_blocks, x_blocks, kj):
    return pl.pallas_call(
        census_kernel,
        out_shape=jax.ShapeDtypeStruct((8, TILE), jnp.float32),
        in_specs=[VMEM] * (ZS + XS + 1),
        out_specs=VMEM,
        compiler_params=pltpu.CompilerParams(vmem_limit_bytes=40 * 2**20),
        name="census",
    )(*a_blocks, *x_blocks, kj)


def per_device(out_weights, in_weights, tile_list, tile_count, owner):
    am, *leaving = prologue(out_weights, in_weights, tile_list, tile_count, owner)
    kj = lax.all_gather(to_lines(am), "row", axis=0, tiled=False)
    owned = [leaving[0]] + [along_row(leaving[e], e) for e in range(1, 4)]
    both = jnp.concatenate(owned, axis=1)
    mine = jnp.concatenate([o[0] for o in owned], axis=0)
    a = {0: mine}
    for s in (1, 7, 2, 6):
        a[s] = along_z(mine, s)
    x = [both] + [along_x(both, r) for r in range(1, XS)]
    a[3] = along_z(a[2], 1)
    a[5] = along_z(a[6], -1)
    a[4] = along_z(a[2], 2)
    part = census([a[s] for s in range(ZS)], x, kj)
    sent = jnp.broadcast_to(part.reshape(1, 1, -1), (COLS, 1, part.size))
    total = lax.all_to_all(sent, "col", 0, 0, tiled=True).sum(axis=0)
    total = total.reshape(2, -1)
    return total[0], total[1]


def solution(mesh):
    in_specs = (P("row", "col"), P("row", "col"), P(), P(), P())
    return jax.shard_map(
        per_device, mesh=mesh, in_specs=in_specs, out_specs=(P("row"), P("row")), check_vma=False
    )
```

```python
import jax
import jax.numpy as jnp
from jax import lax
from jax.experimental import pallas as pl
from jax.experimental.pallas import tpu as pltpu
from jax.sharding import PartitionSpec as P

TILE = 128
XS, ZS, YS, CORES = 4, 8, 8, 2
ROWS, COLS = YS * CORES, XS * ZS
TILES = 4
VMEM = pl.BlockSpec(memory_space=pltpu.VMEM)
SMEM = pl.BlockSpec(memory_space=pltpu.SMEM)


def along_x(a, by):
    pairs = [(x * ZS + z, (x + by) % XS * ZS + z) for x in range(XS) for z in range(ZS)]
    return lax.ppermute(a, "col", pairs)


def along_z(a, by):
    pairs = [(x * ZS + z, x * ZS + (z + by) % ZS) for x in range(XS) for z in range(ZS)]
    return lax.ppermute(a, "col", pairs)


def along_row(a, by):
    return lax.ppermute(a, "row", [(i, (i + by) % ROWS) for i in range(ROWS)])


def along_y(a, by):
    return along_row(a, by * CORES)


def swap_cores(a):
    return lax.ppermute(a, "row", [(i, i ^ 1) for i in range(ROWS)])


def to_lines(a):
    pairs = []
    for y in range(YS):
        for k in range(CORES):
            for x in range(XS):
                for z in range(ZS):
                    src = (y * CORES + k) * COLS + x * ZS + z
                    dst = ((y % 2 * XS + x) * CORES + k) * COLS + y // 2 * ZS + z
                    pairs.append((src, dst))
    return lax.ppermute(a, ("row", "col"), pairs)


def tile_mask(tile_list, tile_count):
    tile_total = tile_list.shape[0]
    live = jnp.arange(tile_list.shape[1], dtype=jnp.int32)[None, :] < tile_count[:, None]
    tiles = jnp.arange(tile_total, dtype=jnp.int32)
    hits = (tile_list[:, :, None] == tiles[None, None, :]) & live[:, :, None]
    return jnp.any(hits, axis=1).astype(jnp.float32)


NEAR, FAR = (0, 1, 7, 2, 6), (3, 5, 4)


def census_kernel(*refs):
    a_refs, x_refs = refs[:ZS], refs[ZS : ZS + XS]
    near, far, near_w, far_w, listed, owner = refs[ZS + XS : ZS + XS + 6]
    e_refs = refs[ZS + XS + 6 : ZS + XS + 6 + TILES]
    a_all, acc, res = refs[ZS + XS + 6 + TILES :]
    row, col = lax.axis_index("row"), lax.axis_index("col")
    my_y, my_k, my_x, my_z = row // CORES, row % CORES, col // ZS, col % ZS

    def kept(ref, lead, row_tile, col_tile, rows, cols):
        out = []
        for t in range(rows):
            line = []
            for q in range(cols):
                tile = ref[(*lead, pl.ds(t * TILE, TILE), pl.ds(q * TILE, TILE))]
                keep = listed(row_tile + t, col_tile + q)
                line.append(tile * jnp.full((TILE, TILE), keep, jnp.float32).astype(tile.dtype))
            out.append(jnp.concatenate(line, axis=1))
        return jnp.concatenate(out, axis=0)

    table = listed
    listed = lambda a, b: table[a, b]
    for s in range(ZS):
        from_z = lax.rem(my_z + ZS - s, ZS)
        a_all[from_z] = kept(a_refs[s], (), row * TILES, 2 * (my_x * ZS + from_z), TILES, 2)
    acc[...] = jnp.zeros_like(acc)
    for swapped in range(CORES):
        from_k = my_k if swapped == 0 else 1 - my_k
        for group, offsets in (((near, near_w)[swapped], NEAR), ((far, far_w)[swapped], FAR)):
            for n, s in enumerate(offsets):
                place = lax.rem(my_y + YS - s, YS)
                from_x = place % XS
                from_z = place // XS * 4 + from_k * 2
                b = kept(group, (n,), 2 * (my_x * ZS + from_z), 2 * (from_x * ZS + my_z), TILES, 2)
                part = jnp.dot(a_all[from_z], b[:256], preferred_element_type=jnp.float32)
                part += jnp.dot(a_all[from_z + 1], b[256:], preferred_element_type=jnp.float32)
                acc[from_x] += part
    trans = cyc = None
    for r in range(XS):
        from_x = lax.rem(my_x + XS - r, XS)
        total = acc[from_x]
        tile = 2 * (from_x * ZS + my_z)
        t = total * kept(x_refs[r], (0,), row * TILES, tile, TILES, 2).astype(jnp.float32)
        listed = lambda a, b: table[b, a]
        c = total * kept(x_refs[r], (1,), row * TILES, tile, TILES, 2).astype(jnp.float32)
        listed = lambda a, b: table[a, b]
        trans = t if trans is None else trans + t
        cyc = c if cyc is None else cyc + c
    for t in range(TILES):
        for which, full in ((0, trans), (1, cyc)):
            tile = full[t * TILE : (t + 1) * TILE, :]
            folded = (tile[:, :TILE] + tile[:, TILE:]).T
            res[2 * t + which : 2 * t + which + 1, :] = jnp.sum(folded, axis=0, keepdims=True)
    for e in range(TILES):
        which = 0
        for t in range(1, TILES):
            offset = lax.rem(owner[row * TILES + t] - row + ROWS, ROWS)
            which = jnp.where(offset == e, t, which)
        e_refs[e][...] = res[pl.ds(2 * which, 2), :]


def census(a_blocks, x_blocks, b_blocks, listed, owner):
    rows, cols = a_blocks[0].shape
    return pl.pallas_call(
        census_kernel,
        out_shape=[jax.ShapeDtypeStruct((2, TILE), jnp.float32)] * TILES,
        in_specs=[VMEM] * (ZS + XS + 4) + [SMEM] * 2,
        out_specs=[VMEM] * TILES,
        scratch_shapes=[
            pltpu.VMEM((ZS, rows, cols), a_blocks[0].dtype),
            pltpu.VMEM((XS, rows, cols), jnp.float32),
            pltpu.VMEM((2 * TILES, TILE), jnp.float32),
        ],
        compiler_params=pltpu.CompilerParams(vmem_limit_bytes=40 * 2**20),
        name="census",
    )(*a_blocks, *x_blocks, *b_blocks, listed, owner)


def gathered(a, along):
    near = {0: a}
    for s in (2, 6, 1, 7):
        near[s] = along(a, s if s < 4 else s - 8)
    far = {3: along(near[2], 1), 5: along(near[6], -1), 4: along(near[2], 2)}
    return near, far


def per_device(out_weights, in_weights, tile_list, tile_count, owner):
    lines = to_lines(out_weights)
    a_near, a_far = gathered(out_weights, along_z)
    a = a_near | a_far
    both = jnp.stack([out_weights, in_weights])
    x = [both] + [along_x(both, r) for r in (1, -1 % XS, 2)]
    x = [x[0], x[1], x[3], x[2]]
    b_near, b_far = gathered(lines, along_y)
    near = jnp.stack([b_near[s] for s in NEAR])
    far = jnp.stack([b_far[s] for s in FAR])
    b = [near, far, swap_cores(near), swap_cores(far)]
    parts = census([a[s] for s in range(ZS)], x, b, tile_mask(tile_list, tile_count), owner)
    owned = [parts[0]] + [along_row(parts[e], e) for e in range(1, TILES)]
    first = jnp.minimum(lax.axis_index("row"), TILES - 1)
    places = [jnp.where(e <= first, first - e, TILES + first - e) for e in range(TILES)]
    ordered = []
    for p in range(TILES):
        ordered.append(sum(jnp.where(places[e] == p, owned[e], 0.0) for e in range(TILES)))
    part = jnp.stack(ordered, axis=1)
    sent = jnp.broadcast_to(part.reshape(1, 1, -1), (COLS, 1, part.size))
    total = lax.all_to_all(sent, "col", 0, 0, tiled=True).sum(axis=0)
    total = total.reshape(2, -1)
    return total[0], total[1]


def solution(mesh):
    in_specs = (P("row", "col"), P("row", "col"), P(), P(), P())
    return jax.shard_map(
        per_device, mesh=mesh, in_specs=in_specs, out_specs=(P("row"), P("row")), check_vma=False
    )
```

```python
import jax
import jax.numpy as jnp
import numpy as np
from jax import lax
from jax.experimental import pallas as pl
from jax.experimental.pallas import tpu as pltpu
from jax.sharding import PartitionSpec as P

TILE = 128
XS, ZS, YS, CORES = 4, 8, 8, 2
ROWS, COLS = YS * CORES, XS * ZS
VMEM = pl.BlockSpec(memory_space=pltpu.VMEM)
SMEM = pl.BlockSpec(memory_space=pltpu.SMEM)


def along_x(a, by):
    pairs = [(x * ZS + z, (x + by) % XS * ZS + z) for x in range(XS) for z in range(ZS)]
    return lax.ppermute(a, "col", pairs)


def along_z(a, by):
    pairs = [(x * ZS + z, x * ZS + (z + by) % ZS) for x in range(XS) for z in range(ZS)]
    return lax.ppermute(a, "col", pairs)


def along_row(a, by):
    return lax.ppermute(a, "row", [(i, (i + by) % ROWS) for i in range(ROWS)])


def to_lines(a):
    pairs = []
    for y in range(YS):
        for k in range(CORES):
            for x in range(XS):
                for z in range(ZS):
                    src = (y * CORES + k) * COLS + x * ZS + z
                    dst = ((y % 2 * XS + x) * CORES + k) * COLS + y // 2 * ZS + z
                    pairs.append((src, dst))
    return lax.ppermute(a, ("row", "col"), pairs)


def prologue_kernel(out_ref, in_ref, list_ref, count_ref, owner_ref, am_ref, *e_refs):
    row, col = lax.axis_index("row"), lax.axis_index("col")
    tiles = out_ref.shape[0] // TILE
    slots, rows_total = list_ref.shape
    lane = lax.broadcasted_iota(jnp.int32, (1, rows_total), 1)
    live = lax.broadcasted_iota(jnp.int32, list_ref.shape, 0) < count_ref[...]

    def rows_with(b):
        hit = (list_ref[...] == b) & live
        return jnp.max(jnp.where(hit, 1.0, 0.0), axis=0, keepdims=True)

    has_col = [rows_with(col * 2 + q) for q in range(2)]
    has_row = [rows_with(row * tiles + t) for t in range(tiles)]

    def listed(vector, a):
        return jnp.max(jnp.where(lane == a, vector, 0.0), axis=1, keepdims=True)

    im_ref = e_refs[-1]
    for t in range(tiles):
        for q in range(2):
            rows, cols = pl.ds(t * TILE, TILE), pl.ds(q * TILE, TILE)
            keep = jnp.broadcast_to(listed(has_col[q], row * tiles + t), (TILE, TILE))
            am_ref[rows, cols] = out_ref[rows, cols] * keep.astype(out_ref.dtype)
            keep = jnp.broadcast_to(listed(has_row[t], col * 2 + q), (TILE, TILE))
            im_ref[rows, cols] = in_ref[rows, cols] * keep.astype(in_ref.dtype)
    for e in range(tiles):
        which = 0
        for t in range(1, tiles):
            offset = lax.rem(owner_ref[row * tiles + t] - row + ROWS, ROWS)
            which = jnp.where(offset == e, t, which)
        rows = pl.ds(pl.multiple_of(which * TILE, TILE), TILE)
        e_refs[e][0] = am_ref[rows, :]
        e_refs[e][1] = im_ref[rows, :]


def prologue(out_block, in_block, tile_list, tile_count, owner):
    rows, cols = out_block.shape
    tiles = rows // TILE
    dtype = out_block.dtype
    one = jax.ShapeDtypeStruct((2, TILE, cols), dtype)
    return pl.pallas_call(
        prologue_kernel,
        out_shape=[jax.ShapeDtypeStruct((rows, cols), dtype)] + [one] * tiles,
        in_specs=[VMEM, VMEM, VMEM, VMEM, SMEM],
        out_specs=[VMEM] * (1 + tiles),
        scratch_shapes=[pltpu.VMEM((rows, cols), dtype)],
        name="prologue",
    )(out_block, in_block, tile_list.T, tile_count[None, :], owner)


def pack_kernel(*refs):
    mine_ref, both_ref = refs[-2:]
    for e, ref in enumerate(refs[:-2]):
        rows = pl.ds(e * TILE, TILE)
        mine_ref[rows, :] = ref[0]
        both_ref[0, rows, :] = ref[0]
        both_ref[1, rows, :] = ref[1]


def pack(owned):
    _, tile, cols = owned[0].shape
    rows, dtype = len(owned) * tile, owned[0].dtype
    return pl.pallas_call(
        pack_kernel,
        out_shape=[
            jax.ShapeDtypeStruct((rows, cols), dtype),
            jax.ShapeDtypeStruct((2, rows, cols), dtype),
        ],
        in_specs=[VMEM] * len(owned),
        out_specs=[VMEM] * 2,
        name="pack",
    )(*owned)


def census_kernel(*refs):
    a_refs, x_refs = refs[:ZS], refs[ZS : ZS + XS]
    kj_ref, res_ref = refs[ZS + XS], refs[ZS + XS + 1]
    row, col = lax.axis_index("row"), lax.axis_index("col")
    my_x, my_z = col // ZS, col % ZS
    tiles = 4
    first = jnp.minimum(row, tiles - 1)
    trans = cyc = None
    for r in range(XS):
        from_x = lax.rem(my_x + XS - r, XS)
        total = None
        for s in range(ZS):
            from_z = lax.rem(my_z + ZS - s, ZS)
            shard = (from_z // 4 * XS + from_x) * CORES + from_z % 4 // 2
            rows = pl.ds(pl.multiple_of(from_z % 2 * 256, 256), 256)
            part = jnp.dot(a_refs[s][...], kj_ref[shard, rows, :], preferred_element_type=jnp.float32)
            total = part if total is None else total + part
        t = total * x_refs[r][0].astype(jnp.float32)
        c = total * x_refs[r][1].astype(jnp.float32)
        trans = t if trans is None else trans + t
        cyc = c if cyc is None else cyc + c
    for e in range(tiles):
        place = jnp.where(e <= first, first - e, tiles + first - e)
        for which, full in ((0, trans), (1, cyc)):
            tile = full[e * TILE : (e + 1) * TILE, :]
            folded = (tile[:, :TILE] + tile[:, TILE:]).T
            res_ref[pl.ds(which * tiles + place, 1), :] = jnp.sum(folded, axis=0, keepdims=True)


def census(a_blocks, x_blocks, kj):
    return pl.pallas_call(
        census_kernel,
        out_shape=jax.ShapeDtypeStruct((8, TILE), jnp.float32),
        in_specs=[VMEM] * (ZS + XS + 1),
        out_specs=VMEM,
        compiler_params=pltpu.CompilerParams(vmem_limit_bytes=12 * 2**20),
        name="census",
    )(*a_blocks, *x_blocks, kj)


def per_device(out_weights, in_weights, tile_list, tile_count, owner):
    am, *leaving = prologue(out_weights, in_weights, tile_list, tile_count, owner)
    lines = to_lines(am)
    owned = [leaving[0]] + [along_row(leaving[e], e) for e in range(1, 4)]
    lines, *owned = lax.optimization_barrier((lines, *owned))
    kj = lax.all_gather(lines, "row", axis=0, tiled=False)
    mine, both = pack(owned)
    a = {0: mine}
    for s in (2, 6, 1, 7):
        a[s] = along_z(mine, s)
    x = [both] + [along_x(both, r) for r in range(1, XS)]
    a[3] = along_z(a[2], 1)
    a[5] = along_z(a[6], -1)
    a[4] = along_z(a[2], 2)
    part = census([a[s] for s in range(ZS)], x, kj)
    sent = jnp.broadcast_to(part.reshape(1, 1, -1), (COLS, 1, part.size))
    total = lax.all_to_all(sent, "col", 0, 0, tiled=True).sum(axis=0)
    total = total.reshape(2, -1)
    return total[0], total[1]


def solution(mesh):
    in_specs = (P("row", "col"), P("row", "col"), P(), P(), P())
    return jax.shard_map(
        per_device, mesh=mesh, in_specs=in_specs, out_specs=(P("row"), P("row")), check_vma=False
    )
```

```python
import jax
import jax.numpy as jnp
from jax import lax
from jax.experimental import pallas as pl
from jax.experimental.pallas import tpu as pltpu
from jax.sharding import PartitionSpec as P

TILE = 128
XS, ZS, YS, CORES = 4, 8, 8, 2
ROWS, COLS = YS * CORES, XS * ZS
TILES = 4
VMEM = pl.BlockSpec(memory_space=pltpu.VMEM)
SMEM = pl.BlockSpec(memory_space=pltpu.SMEM)


def along_x(a, by):
    pairs = [(x * ZS + z, (x + by) % XS * ZS + z) for x in range(XS) for z in range(ZS)]
    return lax.ppermute(a, "col", pairs)


def along_z(a, by):
    pairs = [(x * ZS + z, x * ZS + (z + by) % ZS) for x in range(XS) for z in range(ZS)]
    return lax.ppermute(a, "col", pairs)


def along_row(a, by):
    return lax.ppermute(a, "row", [(i, (i + by) % ROWS) for i in range(ROWS)])


def to_lines(a):
    pairs = []
    for y in range(YS):
        for k in range(CORES):
            for x in range(XS):
                for z in range(ZS):
                    src = (y * CORES + k) * COLS + x * ZS + z
                    dst = ((y % 2 * XS + x) * CORES + k) * COLS + y // 2 * ZS + z
                    pairs.append((src, dst))
    return lax.ppermute(a, ("row", "col"), pairs)


def prologue_kernel(out_ref, in_ref, list_ref, count_ref, am_ref, both_ref):
    row, col = lax.axis_index("row"), lax.axis_index("col")
    tiles = out_ref.shape[0] // TILE
    slots, rows_total = list_ref.shape
    lane = lax.broadcasted_iota(jnp.int32, (1, rows_total), 1)
    live = lax.broadcasted_iota(jnp.int32, list_ref.shape, 0) < count_ref[...]

    def rows_with(b):
        hit = (list_ref[...] == b) & live
        return jnp.max(jnp.where(hit, 1.0, 0.0), axis=0, keepdims=True)

    has_col = [rows_with(col * 2 + q) for q in range(2)]
    has_row = [rows_with(row * tiles + t) for t in range(tiles)]

    def listed(vector, a):
        return jnp.max(jnp.where(lane == a, vector, 0.0), axis=1, keepdims=True)

    for t in range(tiles):
        for q in range(2):
            rows, cols = pl.ds(t * TILE, TILE), pl.ds(q * TILE, TILE)
            keep = jnp.broadcast_to(listed(has_col[q], row * tiles + t), (TILE, TILE))
            kept = out_ref[rows, cols] * keep.astype(out_ref.dtype)
            am_ref[rows, cols] = kept
            both_ref[0, rows, cols] = kept
            keep = jnp.broadcast_to(listed(has_row[t], col * 2 + q), (TILE, TILE))
            both_ref[1, rows, cols] = in_ref[rows, cols] * keep.astype(in_ref.dtype)


def prologue(out_block, in_block, tile_list, tile_count):
    rows, cols = out_block.shape
    dtype = out_block.dtype
    return pl.pallas_call(
        prologue_kernel,
        out_shape=[
            jax.ShapeDtypeStruct((rows, cols), dtype),
            jax.ShapeDtypeStruct((2, rows, cols), dtype),
        ],
        in_specs=[VMEM] * 4,
        out_specs=[VMEM] * 2,
        name="prologue",
    )(out_block, in_block, tile_list.T, tile_count[None, :])


def tile_mask(tile_list, tile_count):
    tile_total = tile_list.shape[0]
    live = jnp.arange(tile_list.shape[1], dtype=jnp.int32)[None, :] < tile_count[:, None]
    tiles = jnp.arange(tile_total, dtype=jnp.int32)
    hits = (tile_list[:, :, None] == tiles[None, None, :]) & live[:, :, None]
    return jnp.any(hits, axis=1).astype(jnp.float32)


def census_kernel(*refs):
    a_refs, x_refs = refs[:ZS], refs[ZS : ZS + XS]
    kj_ref, listed, owner = refs[ZS + XS : ZS + XS + 3]
    e_refs, res = refs[ZS + XS + 3 : -1], refs[-1]
    row, col = lax.axis_index("row"), lax.axis_index("col")
    my_x, my_z = col // ZS, col % ZS
    tiles = 4

    def kept(shard, start, row_tile, col_tile):
        lines = []
        for t in range(2):
            line = []
            for q in range(2):
                rows = pl.ds(pl.multiple_of(start + t * TILE, TILE), TILE)
                tile = kj_ref[shard, rows, q * TILE : (q + 1) * TILE]
                keep = jnp.full((TILE, TILE), listed[row_tile + t, col_tile + q], jnp.float32)
                line.append(tile * keep.astype(tile.dtype))
            lines.append(jnp.concatenate(line, axis=1))
        return jnp.concatenate(lines, axis=0)

    trans = cyc = None
    for r in range(XS):
        from_x = lax.rem(my_x + XS - r, XS)
        total = None
        for s in range(ZS):
            from_z = lax.rem(my_z + ZS - s, ZS)
            shard = (from_z // 4 * XS + from_x) * CORES + from_z % 4 // 2
            tile = 2 * (my_x * ZS + from_z)
            block = kept(shard, from_z % 2 * 256, tile, 2 * (from_x * ZS + my_z))
            part = jnp.dot(a_refs[s][...], block, preferred_element_type=jnp.float32)
            total = part if total is None else total + part
        t = total * x_refs[r][0].astype(jnp.float32)
        c = total * x_refs[r][1].astype(jnp.float32)
        trans = t if trans is None else trans + t
        cyc = c if cyc is None else cyc + c
    for t in range(tiles):
        for which, full in ((0, trans), (1, cyc)):
            tile = full[t * TILE : (t + 1) * TILE, :]
            folded = (tile[:, :TILE] + tile[:, TILE:]).T
            res[2 * t + which : 2 * t + which + 1, :] = jnp.sum(folded, axis=0, keepdims=True)
    for e in range(tiles):
        which = 0
        for t in range(1, tiles):
            offset = lax.rem(owner[row * tiles + t] - row + ROWS, ROWS)
            which = jnp.where(offset == e, t, which)
        e_refs[e][...] = res[pl.ds(2 * which, 2), :]


def census(a_blocks, x_blocks, kj, listed, owner):
    return pl.pallas_call(
        census_kernel,
        out_shape=[jax.ShapeDtypeStruct((2, TILE), jnp.float32)] * TILES,
        in_specs=[VMEM] * (ZS + XS + 1) + [SMEM] * 2,
        out_specs=[VMEM] * TILES,
        scratch_shapes=[pltpu.VMEM((2 * TILES, TILE), jnp.float32)],
        compiler_params=pltpu.CompilerParams(vmem_limit_bytes=12 * 2**20),
        name="census",
    )(*a_blocks, *x_blocks, kj, listed, owner)


def per_device(out_weights, in_weights, tile_list, tile_count, owner):
    kj = lax.all_gather(to_lines(out_weights), "row", axis=0, tiled=False)
    mine, both = prologue(out_weights, in_weights, tile_list, tile_count)
    a = {0: mine}
    for s in (2, 6, 1, 7):
        a[s] = along_z(mine, s)
    x = {0: both, 1: along_x(both, 1)}
    a[4] = along_z(a[2], 2)
    a[5] = along_z(a[6], -1)
    a[3] = along_z(a[2], 1)
    later, a[6], a[2] = lax.optimization_barrier((both, a[6], a[2]))
    x[3] = along_x(later, 3)
    x[2] = along_x(later, 2)
    listed = tile_mask(tile_list, tile_count)
    parts = census([a[s] for s in range(ZS)], [x[r] for r in range(XS)], kj, listed, owner)
    owned = [parts[0]] + [along_row(parts[e], e) for e in range(1, TILES)]
    first = jnp.minimum(lax.axis_index("row"), TILES - 1)
    places = [jnp.where(e <= first, first - e, TILES + first - e) for e in range(TILES)]
    ordered = []
    for p in range(TILES):
        ordered.append(sum(jnp.where(places[e] == p, owned[e], 0.0) for e in range(TILES)))
    part = jnp.stack(ordered, axis=1)
    sent = jnp.broadcast_to(part.reshape(1, 1, -1), (COLS, 1, part.size))
    total = lax.all_to_all(sent, "col", 0, 0, tiled=True).sum(axis=0)
    total = total.reshape(2, -1)
    return total[0], total[1]


def solution(mesh):
    in_specs = (P("row", "col"), P("row", "col"), P(), P(), P())
    return jax.shard_map(
        per_device, mesh=mesh, in_specs=in_specs, out_specs=(P("row"), P("row")), check_vma=False
    )
```

```python
import jax
import jax.numpy as jnp
from jax import lax
from jax.experimental import pallas as pl
from jax.experimental.pallas import tpu as pltpu
from jax.sharding import PartitionSpec as P

TILE = 128
XS, ZS, YS, CORES = 4, 8, 8, 2
ROWS, COLS = YS * CORES, XS * ZS
TILES = 4
VMEM = pl.BlockSpec(memory_space=pltpu.VMEM)
SMEM = pl.BlockSpec(memory_space=pltpu.SMEM)


def along_x(a, by):
    pairs = [(x * ZS + z, (x + by) % XS * ZS + z) for x in range(XS) for z in range(ZS)]
    return lax.ppermute(a, "col", pairs)


def along_row(a, by):
    return lax.ppermute(a, "row", [(i, (i + by) % ROWS) for i in range(ROWS)])


def along_y(a, by):
    return along_row(a, by * CORES)


def swap_cores(a):
    return lax.ppermute(a, "row", [(i, i ^ 1) for i in range(ROWS)])


def to_lines(a):
    pairs = []
    for y in range(YS):
        for k in range(CORES):
            for x in range(XS):
                for z in range(ZS):
                    b = y // 2
                    away = (3, 2, 0, 1)[(x - b) % XS]
                    to_y = (y + away if y % 2 else y - away) % YS
                    src = (y * CORES + k) * COLS + x * ZS + z
                    dst = (to_y * CORES + k) * COLS + b * ZS + z
                    pairs.append((src, dst))
    return lax.ppermute(a, ("row", "col"), pairs)


def sent_from(y, b):
    ahead = lax.rem(y - 2 * b - 1 + 2 * YS, YS)
    odd = jnp.where(ahead < YS // 2, 1, 0)
    away = jnp.where(odd == 1, ahead, YS - 1 - ahead)
    x = lax.rem(b + jnp.where(away < 2, away + 2, 3 - away), XS)
    return odd, x


def all_along_z(a):
    groups = [[x * ZS + z for z in range(ZS)] for x in range(XS)]
    return lax.all_gather(a, "col", axis=0, tiled=False, axis_index_groups=groups)


NEAR, FAR = (0, 2, 6, 1, 7), (4, 5, 3)


def prologue_kernel(out_ref, in_ref, list_ref, count_ref, am_ref, both_ref):
    row, col = lax.axis_index("row"), lax.axis_index("col")
    tiles = out_ref.shape[0] // TILE
    slots, rows_total = list_ref.shape
    lane = lax.broadcasted_iota(jnp.int32, (1, rows_total), 1)
    live = lax.broadcasted_iota(jnp.int32, list_ref.shape, 0) < count_ref[...]

    def rows_with(b):
        hit = (list_ref[...] == b) & live
        return jnp.max(jnp.where(hit, 1.0, 0.0), axis=0, keepdims=True)

    has_col = [rows_with(col * 2 + q) for q in range(2)]
    has_row = [rows_with(row * tiles + t) for t in range(tiles)]

    def listed(vector, a):
        return jnp.max(jnp.where(lane == a, vector, 0.0), axis=1, keepdims=True)

    for t in range(tiles):
        for q in range(2):
            rows, cols = pl.ds(t * TILE, TILE), pl.ds(q * TILE, TILE)
            keep = jnp.broadcast_to(listed(has_col[q], row * tiles + t), (TILE, TILE))
            kept = out_ref[rows, cols] * keep.astype(out_ref.dtype)
            am_ref[rows, cols] = kept
            both_ref[0, rows, cols] = kept
            keep = jnp.broadcast_to(listed(has_row[t], col * 2 + q), (TILE, TILE))
            both_ref[1, rows, cols] = in_ref[rows, cols] * keep.astype(in_ref.dtype)


def prologue(out_block, in_block, tile_list, tile_count):
    rows, cols = out_block.shape
    dtype = out_block.dtype
    return pl.pallas_call(
        prologue_kernel,
        out_shape=[
            jax.ShapeDtypeStruct((rows, cols), dtype),
            jax.ShapeDtypeStruct((2, rows, cols), dtype),
        ],
        in_specs=[VMEM] * 4,
        out_specs=[VMEM] * 2,
        name="prologue",
    )(out_block, in_block, tile_list.T, tile_count[None, :])


def tile_mask(tile_list, tile_count):
    tile_total = tile_list.shape[0]
    live = jnp.arange(tile_list.shape[1], dtype=jnp.int32)[None, :] < tile_count[:, None]
    tiles = jnp.arange(tile_total, dtype=jnp.int32)
    hits = (tile_list[:, :, None] == tiles[None, None, :]) & live[:, :, None]
    return jnp.any(hits, axis=1).astype(jnp.float32)


def census_kernel(*refs):
    a_ref, x_refs = refs[0], refs[1 : 1 + XS]
    near, far, near_w, far_w, listed, owner = refs[1 + XS : 7 + XS]
    e_refs, acc, res = refs[7 + XS : -2], refs[-2], refs[-1]
    row, col = lax.axis_index("row"), lax.axis_index("col")
    my_y, my_k, my_x, my_z = row // CORES, row % CORES, col // ZS, col % ZS
    tiles = TILES

    def kept(ref, n, start, row_tile, col_tile):
        lines = []
        for t in range(2):
            line = []
            for q in range(2):
                rows = slice(start + t * TILE, start + (t + 1) * TILE)
                tile = ref[n, rows, q * TILE : (q + 1) * TILE]
                keep = jnp.full((TILE, TILE), listed[row_tile + t, col_tile + q], jnp.float32)
                line.append(tile * keep.astype(tile.dtype))
            lines.append(jnp.concatenate(line, axis=1))
        return jnp.concatenate(lines, axis=0)

    acc[...] = jnp.zeros_like(acc)
    for swapped, groups in ((0, (near, far)), (1, (near_w, far_w))):
        from_k = lax.rem(my_k + swapped, CORES)
        for group, offsets in zip(groups, (NEAR, FAR)):
            for n, s in enumerate(offsets):
                odd, from_x = sent_from(lax.rem(my_y + YS - s, YS), my_x)
                from_z = odd * 4 + from_k * 2
                row_tile, col_tile = 2 * (my_x * ZS + from_z), 2 * (from_x * ZS + my_z)
                upper = kept(group, n, 0, row_tile, col_tile)
                lower = kept(group, n, 256, row_tile + 2, col_tile)
                part = jnp.dot(a_ref[from_z], upper, preferred_element_type=jnp.float32)
                part += jnp.dot(a_ref[from_z + 1], lower, preferred_element_type=jnp.float32)
                acc[from_x] += part
    trans = cyc = None
    for r in range(XS):
        total = acc[lax.rem(my_x + XS - r, XS)]
        t = total * x_refs[r][0].astype(jnp.float32)
        c = total * x_refs[r][1].astype(jnp.float32)
        trans = t if trans is None else trans + t
        cyc = c if cyc is None else cyc + c
    for t in range(tiles):
        for which, full in ((0, trans), (1, cyc)):
            tile = full[t * TILE : (t + 1) * TILE, :]
            folded = (tile[:, :TILE] + tile[:, TILE:]).T
            res[2 * t + which : 2 * t + which + 1, :] = jnp.sum(folded, axis=0, keepdims=True)
    for e in range(tiles):
        which = 0
        for t in range(1, tiles):
            offset = lax.rem(owner[row * tiles + t] - row + ROWS, ROWS)
            which = jnp.where(offset == e, t, which)
        e_refs[e][...] = res[pl.ds(2 * which, 2), :]


def census(a, x_blocks, b_blocks, listed, owner):
    _, rows, cols = a.shape
    return pl.pallas_call(
        census_kernel,
        out_shape=[jax.ShapeDtypeStruct((2, TILE), jnp.float32)] * TILES,
        in_specs=[VMEM] * (1 + XS + 4) + [SMEM] * 2,
        out_specs=[VMEM] * TILES,
        scratch_shapes=[
            pltpu.VMEM((XS, rows, cols), jnp.float32),
            pltpu.VMEM((2 * TILES, TILE), jnp.float32),
        ],
        compiler_params=pltpu.CompilerParams(vmem_limit_bytes=12 * 2**20),
        name="census",
    )(a, *x_blocks, *b_blocks, listed, owner)


def per_device(out_weights, in_weights, tile_list, tile_count, owner):
    lines = to_lines(out_weights)
    mine, both = prologue(out_weights, in_weights, tile_list, tile_count)
    a = all_along_z(mine)
    x = {0: both, 1: along_x(both, 1)}
    lines, x[1] = lax.optimization_barrier((lines, x[1]))
    b = {0: lines}
    for s in (2, 6, 1, 7):
        b[s] = along_y(lines, s if s < 4 else s - YS)
    x[3] = along_x(both, 3)
    b[6], x[3] = lax.optimization_barrier((b[6], x[3]))
    b[4] = along_y(b[2], 2)
    b[5] = along_y(b[6], -1)
    b[3] = along_y(b[2], 1)
    x[2] = along_x(both, 2)
    b[7], x[2] = lax.optimization_barrier((b[7], x[2]))
    near = jnp.stack([b[s] for s in NEAR])
    far = jnp.stack([b[s] for s in FAR])
    blocks = [near, far, swap_cores(near), swap_cores(far)]
    listed = tile_mask(tile_list, tile_count)
    parts = census(a, [x[r] for r in range(XS)], blocks, listed, owner)
    owned = [parts[0]] + [along_row(parts[e], e) for e in range(1, TILES)]
    first = jnp.minimum(lax.axis_index("row"), TILES - 1)
    places = [jnp.where(e <= first, first - e, TILES + first - e) for e in range(TILES)]
    ordered = []
    for p in range(TILES):
        ordered.append(sum(jnp.where(places[e] == p, owned[e], 0.0) for e in range(TILES)))
    part = jnp.stack(ordered, axis=1)
    sent = jnp.broadcast_to(part.reshape(1, 1, -1), (COLS, 1, part.size))
    total = lax.all_to_all(sent, "col", 0, 0, tiled=True).sum(axis=0)
    total = total.reshape(2, -1)
    return total[0], total[1]


def solution(mesh):
    in_specs = (P("row", "col"), P("row", "col"), P(), P(), P())
    return jax.shard_map(
        per_device, mesh=mesh, in_specs=in_specs, out_specs=(P("row"), P("row")), check_vma=False
    )
```

```python
import jax
import jax.numpy as jnp
from jax import lax
from jax.experimental import pallas as pl
from jax.experimental.pallas import tpu as pltpu
from jax.sharding import PartitionSpec as P

TILE = 128
XS, ZS, YS, CORES = 4, 8, 8, 2
ROWS, COLS = YS * CORES, XS * ZS
VMEM = pl.BlockSpec(memory_space=pltpu.VMEM)
SMEM = pl.BlockSpec(memory_space=pltpu.SMEM)


def along_x(a, by):
    pairs = [(x * ZS + z, (x + by) % XS * ZS + z) for x in range(XS) for z in range(ZS)]
    return lax.ppermute(a, "col", pairs)


def along_z(a, by):
    pairs = [(x * ZS + z, x * ZS + (z + by) % ZS) for x in range(XS) for z in range(ZS)]
    return lax.ppermute(a, "col", pairs)


def along_row(a, by):
    return lax.ppermute(a, "row", [(i, (i + by) % ROWS) for i in range(ROWS)])


AWAY = (3, 2, 0, 1)


def to_lines(a):
    pairs = []
    for y in range(YS):
        for k in range(CORES):
            for x in range(XS):
                for z in range(ZS):
                    b = y // 2
                    away = AWAY[(x - b) % XS]
                    to_y = (y + away if y % 2 else y - away) % YS
                    src = (y * CORES + k) * COLS + x * ZS + z
                    dst = (to_y * CORES + k) * COLS + b * ZS + z
                    pairs.append((src, dst))
    return lax.ppermute(a, ("row", "col"), pairs)


def line_row(odd, x, b):
    ahead = lax.rem(x - b + XS, XS)
    away = jnp.where(ahead < 2, 3 - ahead, ahead - 2)
    return lax.rem(2 * b + odd * (1 + 2 * away) - away + YS, YS)


def prologue_kernel(out_ref, in_ref, list_ref, count_ref, owner_ref, am_ref, *e_refs):
    row, col = lax.axis_index("row"), lax.axis_index("col")
    tiles = out_ref.shape[0] // TILE
    slots, rows_total = list_ref.shape
    lane = lax.broadcasted_iota(jnp.int32, (1, rows_total), 1)
    live = lax.broadcasted_iota(jnp.int32, list_ref.shape, 0) < count_ref[...]

    def rows_with(b):
        hit = (list_ref[...] == b) & live
        return jnp.max(jnp.where(hit, 1.0, 0.0), axis=0, keepdims=True)

    has_col = [rows_with(col * 2 + q) for q in range(2)]
    has_row = [rows_with(row * tiles + t) for t in range(tiles)]

    def listed(vector, a):
        return jnp.max(jnp.where(lane == a, vector, 0.0), axis=1, keepdims=True)

    im_ref = e_refs[-1]
    for t in range(tiles):
        for q in range(2):
            rows, cols = pl.ds(t * TILE, TILE), pl.ds(q * TILE, TILE)
            keep = jnp.broadcast_to(listed(has_col[q], row * tiles + t), (TILE, TILE))
            am_ref[rows, cols] = out_ref[rows, cols] * keep.astype(out_ref.dtype)
            keep = jnp.broadcast_to(listed(has_row[t], col * 2 + q), (TILE, TILE))
            im_ref[rows, cols] = in_ref[rows, cols] * keep.astype(in_ref.dtype)
    for e in range(tiles):
        which = 0
        for t in range(1, tiles):
            offset = lax.rem(owner_ref[row * tiles + t] - row + ROWS, ROWS)
            which = jnp.where(offset == e, t, which)
        rows = pl.ds(pl.multiple_of(which * TILE, TILE), TILE)
        e_refs[e][0] = am_ref[rows, :]
        e_refs[e][1] = im_ref[rows, :]


def prologue(out_block, in_block, tile_list, tile_count, owner):
    rows, cols = out_block.shape
    tiles = rows // TILE
    dtype = out_block.dtype
    one = jax.ShapeDtypeStruct((2, TILE, cols), dtype)
    return pl.pallas_call(
        prologue_kernel,
        out_shape=[jax.ShapeDtypeStruct((rows, cols), dtype)] + [one] * tiles,
        in_specs=[VMEM, VMEM, VMEM, VMEM, SMEM],
        out_specs=[VMEM] * (1 + tiles),
        scratch_shapes=[pltpu.VMEM((rows, cols), dtype)],
        name="prologue",
    )(out_block, in_block, tile_list.T, tile_count[None, :], owner)


def pack_kernel(*refs):
    mine_ref, both_ref = refs[-2:]
    for e, ref in enumerate(refs[:-2]):
        rows = pl.ds(e * TILE, TILE)
        mine_ref[rows, :] = ref[0]
        both_ref[0, rows, :] = ref[0]
        both_ref[1, rows, :] = ref[1]


def pack(owned):
    _, tile, cols = owned[0].shape
    rows, dtype = len(owned) * tile, owned[0].dtype
    return pl.pallas_call(
        pack_kernel,
        out_shape=[
            jax.ShapeDtypeStruct((rows, cols), dtype),
            jax.ShapeDtypeStruct((2, rows, cols), dtype),
        ],
        in_specs=[VMEM] * len(owned),
        out_specs=[VMEM] * 2,
        name="pack",
    )(*owned)


def census_kernel(*refs):
    a_refs, x_refs = refs[: ZS + 1], refs[ZS + 1 : ZS + XS + 2]
    kj_ref, res_ref = refs[ZS + XS + 2 :]

    def rows_at(s):
        if s == ZS // 2:
            return jnp.concatenate([a_refs[s][...], a_refs[ZS][...]], axis=0)
        return a_refs[s][...]

    def weights_at(r):
        if r == XS // 2:
            return x_refs[r][...], x_refs[XS][...]
        return x_refs[r][0], x_refs[r][1]

    row, col = lax.axis_index("row"), lax.axis_index("col")
    my_x, my_z = col // ZS, col % ZS
    tiles = 4
    first = jnp.minimum(row, tiles - 1)
    trans = cyc = None
    for r in range(XS):
        from_x = lax.rem(my_x + XS - r, XS)
        total = None
        for s in range(ZS):
            from_z = lax.rem(my_z + ZS - s, ZS)
            shard = line_row(from_z // 4, from_x, my_x) * CORES + from_z % 4 // 2
            rows = pl.ds(pl.multiple_of(from_z % 2 * 256, 256), 256)
            part = jnp.dot(rows_at(s), kj_ref[shard, rows, :], preferred_element_type=jnp.float32)
            total = part if total is None else total + part
        out_w, in_w = weights_at(r)
        t = total * out_w.astype(jnp.float32)
        c = total * in_w.astype(jnp.float32)
        trans = t if trans is None else trans + t
        cyc = c if cyc is None else cyc + c
    for e in range(tiles):
        place = jnp.where(e <= first, first - e, tiles + first - e)
        for which, full in ((0, trans), (1, cyc)):
            tile = full[e * TILE : (e + 1) * TILE, :]
            folded = (tile[:, :TILE] + tile[:, TILE:]).T
            res_ref[pl.ds(which * tiles + place, 1), :] = jnp.sum(folded, axis=0, keepdims=True)


def census(a_blocks, x_blocks, kj):
    return pl.pallas_call(
        census_kernel,
        out_shape=jax.ShapeDtypeStruct((8, TILE), jnp.float32),
        in_specs=[VMEM] * (len(a_blocks) + len(x_blocks) + 1),
        out_specs=VMEM,
        compiler_params=pltpu.CompilerParams(vmem_limit_bytes=12 * 2**20),
        name="census",
    )(*a_blocks, *x_blocks, kj)


def per_device(out_weights, in_weights, tile_list, tile_count, owner):
    am, *leaving = prologue(out_weights, in_weights, tile_list, tile_count, owner)
    lines = to_lines(am)
    owned = [leaving[0]] + [along_row(leaving[e], e) for e in range(1, 4)]
    lines, owned[1] = lax.optimization_barrier((lines, owned[1]))
    kj = lax.all_gather(lines, "row", axis=0, tiled=False)
    mine, both = pack(owned)
    half = mine.shape[0] // 2
    a = {0: mine}
    for s in (2, 6):
        a[s] = along_z(mine, s)
    x = {0: both, 1: along_x(both, 1), 3: along_x(both, 3)}
    for s in (1, 7):
        a[s] = along_z(mine, s)
    a[4] = along_z(a[2][:half], 2)
    a[ZS] = along_z(a[6][half:], -2)
    a[3] = along_z(a[2], 1)
    a[5] = along_z(a[6], -1)
    x[2] = along_x(x[1][0], 1)
    x[XS] = along_x(x[3][1], -1)
    part = census([a[s] for s in range(ZS + 1)], [x[r] for r in range(XS + 1)], kj)
    sent = jnp.broadcast_to(part.reshape(1, 1, -1), (COLS, 1, part.size))
    total = lax.all_to_all(sent, "col", 0, 0, tiled=True).sum(axis=0)
    total = total.reshape(2, -1)
    return total[0], total[1]


def solution(mesh):
    in_specs = (P("row", "col"), P("row", "col"), P(), P(), P())
    return jax.shard_map(
        per_device, mesh=mesh, in_specs=in_specs, out_specs=(P("row"), P("row")), check_vma=False
    )
```

```python
import jax
import jax.numpy as jnp
from jax import lax
from jax.experimental import pallas as pl
from jax.experimental.pallas import tpu as pltpu
from jax.sharding import PartitionSpec as P

TILE = 128
XS, ZS, YS, CORES = 4, 8, 8, 2
ROWS, COLS = YS * CORES, XS * ZS
VMEM = pl.BlockSpec(memory_space=pltpu.VMEM)
SMEM = pl.BlockSpec(memory_space=pltpu.SMEM)


def along_x(a, by):
    pairs = [(x * ZS + z, (x + by) % XS * ZS + z) for x in range(XS) for z in range(ZS)]
    return lax.ppermute(a, "col", pairs)


def along_z(a, by):
    pairs = [(x * ZS + z, x * ZS + (z + by) % ZS) for x in range(XS) for z in range(ZS)]
    return lax.ppermute(a, "col", pairs)


def along_row(a, by):
    return lax.ppermute(a, "row", [(i, (i + by) % ROWS) for i in range(ROWS)])


AWAY = (3, 2, 0, 1)


def to_lines(a):
    pairs = []
    for y in range(YS):
        for k in range(CORES):
            for x in range(XS):
                for z in range(ZS):
                    b = y // 2
                    away = AWAY[(x - b) % XS]
                    to_y = (y + away if y % 2 else y - away) % YS
                    src = (y * CORES + k) * COLS + x * ZS + z
                    dst = (to_y * CORES + k) * COLS + b * ZS + z
                    pairs.append((src, dst))
    return lax.ppermute(a, ("row", "col"), pairs)


def line_row(odd, x, b):
    ahead = lax.rem(x - b + XS, XS)
    away = jnp.where(ahead < 2, 3 - ahead, ahead - 2)
    return lax.rem(2 * b + odd * (1 + 2 * away) - away + YS, YS)


def prologue_kernel(out_ref, in_ref, list_ref, count_ref, owner_ref, am_ref, *e_refs):
    row, col = lax.axis_index("row"), lax.axis_index("col")
    tiles = out_ref.shape[0] // TILE
    slots, rows_total = list_ref.shape
    lane = lax.broadcasted_iota(jnp.int32, (1, rows_total), 1)
    live = lax.broadcasted_iota(jnp.int32, list_ref.shape, 0) < count_ref[...]

    def rows_with(b):
        hit = (list_ref[...] == b) & live
        return jnp.max(jnp.where(hit, 1.0, 0.0), axis=0, keepdims=True)

    has_col = [rows_with(col * 2 + q) for q in range(2)]
    has_row = [rows_with(row * tiles + t) for t in range(tiles)]

    def listed(vector, a):
        return jnp.max(jnp.where(lane == a, vector, 0.0), axis=1, keepdims=True)

    im_ref = e_refs[-1]
    for t in range(tiles):
        for q in range(2):
            rows, cols = pl.ds(t * TILE, TILE), pl.ds(q * TILE, TILE)
            keep = jnp.broadcast_to(listed(has_col[q], row * tiles + t), (TILE, TILE))
            am_ref[rows, cols] = out_ref[rows, cols] * keep.astype(out_ref.dtype)
            keep = jnp.broadcast_to(listed(has_row[t], col * 2 + q), (TILE, TILE))
            im_ref[rows, cols] = in_ref[rows, cols] * keep.astype(in_ref.dtype)
    for e in range(tiles):
        which = 0
        for t in range(1, tiles):
            offset = lax.rem(owner_ref[row * tiles + t] - row + ROWS, ROWS)
            which = jnp.where(offset == e, t, which)
        rows = pl.ds(pl.multiple_of(which * TILE, TILE), TILE)
        e_refs[e][0] = am_ref[rows, :]
        e_refs[e][1] = im_ref[rows, :]


def prologue(out_block, in_block, tile_list, tile_count, owner):
    rows, cols = out_block.shape
    tiles = rows // TILE
    dtype = out_block.dtype
    one = jax.ShapeDtypeStruct((2, TILE, cols), dtype)
    return pl.pallas_call(
        prologue_kernel,
        out_shape=[jax.ShapeDtypeStruct((rows, cols), dtype)] + [one] * tiles,
        in_specs=[VMEM, VMEM, VMEM, VMEM, SMEM],
        out_specs=[VMEM] * (1 + tiles),
        scratch_shapes=[pltpu.VMEM((rows, cols), dtype)],
        name="prologue",
    )(out_block, in_block, tile_list.T, tile_count[None, :], owner)


def pack_kernel(*refs):
    mine_ref, both_ref = refs[-2:]
    for e, ref in enumerate(refs[:-2]):
        rows = pl.ds(e * TILE, TILE)
        mine_ref[rows, :] = ref[0]
        both_ref[0, rows, :] = ref[0]
        both_ref[1, rows, :] = ref[1]


def pack(owned):
    _, tile, cols = owned[0].shape
    rows, dtype = len(owned) * tile, owned[0].dtype
    return pl.pallas_call(
        pack_kernel,
        out_shape=[
            jax.ShapeDtypeStruct((rows, cols), dtype),
            jax.ShapeDtypeStruct((2, rows, cols), dtype),
        ],
        in_specs=[VMEM] * len(owned),
        out_specs=[VMEM] * 2,
        name="pack",
    )(*owned)


def census_kernel(*refs):
    a_refs, x_refs = refs[:ZS], refs[ZS : ZS + XS]
    kj_ref, res_ref = refs[ZS + XS], refs[ZS + XS + 1]
    row, col = lax.axis_index("row"), lax.axis_index("col")
    my_x, my_z = col // ZS, col % ZS
    tiles = 4
    first = jnp.minimum(row, tiles - 1)
    trans = cyc = None
    for r in range(XS):
        from_x = lax.rem(my_x + XS - r, XS)
        total = None
        for s in range(ZS):
            from_z = lax.rem(my_z + ZS - s, ZS)
            shard = line_row(from_z // 4, from_x, my_x) * CORES + from_z % 4 // 2
            rows = pl.ds(pl.multiple_of(from_z % 2 * 256, 256), 256)
            part = jnp.dot(a_refs[s][...], kj_ref[shard, rows, :], preferred_element_type=jnp.float32)
            total = part if total is None else total + part
        t = total * x_refs[r][0].astype(jnp.float32)
        c = total * x_refs[r][1].astype(jnp.float32)
        trans = t if trans is None else trans + t
        cyc = c if cyc is None else cyc + c
    for e in range(tiles):
        place = jnp.where(e <= first, first - e, tiles + first - e)
        for which, full in ((0, trans), (1, cyc)):
            tile = full[e * TILE : (e + 1) * TILE, :]
            folded = (tile[:, :TILE] + tile[:, TILE:]).T
            res_ref[pl.ds(which * tiles + place, 1), :] = jnp.sum(folded, axis=0, keepdims=True)


def census(a_blocks, x_blocks, kj):
    return pl.pallas_call(
        census_kernel,
        out_shape=jax.ShapeDtypeStruct((8, TILE), jnp.float32),
        in_specs=[VMEM] * (ZS + XS + 1),
        out_specs=VMEM,
        compiler_params=pltpu.CompilerParams(vmem_limit_bytes=12 * 2**20),
        name="census",
    )(*a_blocks, *x_blocks, kj)


def per_device(out_weights, in_weights, tile_list, tile_count, owner):
    am, *leaving = prologue(out_weights, in_weights, tile_list, tile_count, owner)
    lines = to_lines(am)
    owned = [leaving[0]] + [along_row(leaving[e], e) for e in range(1, 4)]
    lines, *owned = lax.optimization_barrier((lines, *owned))
    kj = lax.all_gather(lines, "row", axis=0, tiled=False)
    mine, both = pack(owned)
    a = {0: mine}
    for s in range(1, ZS // 2):
        a[s] = along_z(a[s - 1], 1)
        a[ZS - s] = along_z(a[(ZS - s + 1) % ZS], -1)
    a[ZS // 2] = along_z(a[ZS // 2 - 1], 1)
    x = [both] + [along_x(both, r) for r in range(1, XS)]
    part = census([a[s] for s in range(ZS)], x, kj)
    sent = jnp.broadcast_to(part.reshape(1, 1, -1), (COLS, 1, part.size))
    total = lax.all_to_all(sent, "col", 0, 0, tiled=True).sum(axis=0)
    total = total.reshape(2, -1)
    return total[0], total[1]


def solution(mesh):
    in_specs = (P("row", "col"), P("row", "col"), P(), P(), P())
    return jax.shard_map(
        per_device, mesh=mesh, in_specs=in_specs, out_specs=(P("row"), P("row")), check_vma=False
    )
```

```python
import jax
import jax.numpy as jnp
from jax import lax
from jax.experimental import pallas as pl
from jax.experimental.pallas import tpu as pltpu
from jax.sharding import PartitionSpec as P

TILE = 128
XS, ZS, YS, CORES = 4, 8, 8, 2
ROWS, COLS = YS * CORES, XS * ZS
HBM = pl.BlockSpec(memory_space=pltpu.HBM)
VMEM = pl.BlockSpec(memory_space=pltpu.VMEM)
SMEM = pl.BlockSpec(memory_space=pltpu.SMEM)


def along_x(a, by):
    pairs = [(x * ZS + z, (x + by) % XS * ZS + z) for x in range(XS) for z in range(ZS)]
    return lax.ppermute(a, "col", pairs)


def along_z(a, by):
    pairs = [(x * ZS + z, x * ZS + (z + by) % ZS) for x in range(XS) for z in range(ZS)]
    return lax.ppermute(a, "col", pairs)


def along_row(a, by):
    return lax.ppermute(a, "row", [(i, (i + by) % ROWS) for i in range(ROWS)])


AWAY = (3, 2, 0, 1)


def to_lines(a):
    pairs = []
    for y in range(YS):
        for k in range(CORES):
            for x in range(XS):
                for z in range(ZS):
                    b = y // 2
                    away = AWAY[(x - b) % XS]
                    to_y = (y + away if y % 2 else y - away) % YS
                    src = (y * CORES + k) * COLS + x * ZS + z
                    dst = (to_y * CORES + k) * COLS + b * ZS + z
                    pairs.append((src, dst))
    return lax.ppermute(a, ("row", "col"), pairs)


def line_row(odd, x, b):
    ahead = lax.rem(x - b + XS, XS)
    away = jnp.where(ahead < 2, 3 - ahead, ahead - 2)
    return lax.rem(2 * b + odd * (1 + 2 * away) - away + YS, YS)


def prologue_kernel(out_ref, in_ref, list_ref, count_ref, owner_ref, am_ref, *e_refs):
    row, col = lax.axis_index("row"), lax.axis_index("col")
    tiles = out_ref.shape[0] // TILE
    slots, rows_total = list_ref.shape
    lane = lax.broadcasted_iota(jnp.int32, (1, rows_total), 1)
    live = lax.broadcasted_iota(jnp.int32, list_ref.shape, 0) < count_ref[...]

    def rows_with(b):
        hit = (list_ref[...] == b) & live
        return jnp.max(jnp.where(hit, 1.0, 0.0), axis=0, keepdims=True)

    has_col = [rows_with(col * 2 + q) for q in range(2)]
    has_row = [rows_with(row * tiles + t) for t in range(tiles)]

    def listed(vector, a):
        return jnp.max(jnp.where(lane == a, vector, 0.0), axis=1, keepdims=True)

    im_ref = e_refs[-1]
    for t in range(tiles):
        for q in range(2):
            rows, cols = pl.ds(t * TILE, TILE), pl.ds(q * TILE, TILE)
            keep = jnp.broadcast_to(listed(has_col[q], row * tiles + t), (TILE, TILE))
            am_ref[rows, cols] = out_ref[rows, cols] * keep.astype(out_ref.dtype)
            keep = jnp.broadcast_to(listed(has_row[t], col * 2 + q), (TILE, TILE))
            im_ref[rows, cols] = in_ref[rows, cols] * keep.astype(in_ref.dtype)
    for e in range(tiles):
        which = 0
        for t in range(1, tiles):
            offset = lax.rem(owner_ref[row * tiles + t] - row + ROWS, ROWS)
            which = jnp.where(offset == e, t, which)
        rows = pl.ds(pl.multiple_of(which * TILE, TILE), TILE)
        e_refs[e][0] = am_ref[rows, :]
        e_refs[e][1] = im_ref[rows, :]


def prologue(out_block, in_block, tile_list, tile_count, owner):
    rows, cols = out_block.shape
    tiles = rows // TILE
    dtype = out_block.dtype
    one = jax.ShapeDtypeStruct((2, TILE, cols), dtype)
    return pl.pallas_call(
        prologue_kernel,
        out_shape=[jax.ShapeDtypeStruct((rows, cols), dtype)] + [one] * tiles,
        in_specs=[VMEM, VMEM, VMEM, VMEM, SMEM],
        out_specs=[VMEM] * (1 + tiles),
        scratch_shapes=[pltpu.VMEM((rows, cols), dtype)],
        name="prologue",
    )(out_block, in_block, tile_list.T, tile_count[None, :], owner)


def pack_kernel(*refs):
    mine_ref, both_ref = refs[-2:]
    for e, ref in enumerate(refs[:-2]):
        rows = pl.ds(e * TILE, TILE)
        mine_ref[rows, :] = ref[0]
        both_ref[0, rows, :] = ref[0]
        both_ref[1, rows, :] = ref[1]


def pack(owned):
    _, tile, cols = owned[0].shape
    rows, dtype = len(owned) * tile, owned[0].dtype
    return pl.pallas_call(
        pack_kernel,
        out_shape=[
            jax.ShapeDtypeStruct((rows, cols), dtype),
            jax.ShapeDtypeStruct((2, rows, cols), dtype),
        ],
        in_specs=[VMEM] * len(owned),
        out_specs=[VMEM] * 2,
        name="pack",
    )(*owned)


def census_kernel(*refs):
    a_refs, x_refs = list(refs[:ZS]), list(refs[ZS : ZS + XS])
    kj_ref, res_ref, a_own, x_own, kj_own, own_sem, kj_sem = refs[ZS + XS :]
    row, col = lax.axis_index("row"), lax.axis_index("col")
    my_x, my_z = col // ZS, col % ZS
    tiles = 4
    first = jnp.minimum(row, tiles - 1)
    own = [
        pltpu.make_async_copy(a_refs[0], a_own, own_sem.at[0]),
        pltpu.make_async_copy(x_refs[0], x_own, own_sem.at[1]),
    ]
    shards = []
    for r in range(XS):
        from_x = lax.rem(my_x + XS - r, XS)
        for n in range(2 * CORES):
            shard = line_row(n // CORES, from_x, my_x) * CORES + n % CORES
            slot = r * 2 * CORES + n
            shards.append(
                pltpu.make_async_copy(kj_ref.at[shard], kj_own.at[slot], kj_sem.at[slot])
            )
    own[0].start()
    for copy in shards[: 2 * CORES]:
        copy.start()
    own[1].start()
    for copy in shards[2 * CORES :]:
        copy.start()
    a_refs[0], x_refs[0] = a_own, x_own
    own[0].wait()
    trans = cyc = None
    for r in range(XS):
        for copy in shards[r * 2 * CORES : (r + 1) * 2 * CORES]:
            copy.wait()
        total = None
        for s in range(ZS):
            from_z = lax.rem(my_z + ZS - s, ZS)
            rows = pl.ds(pl.multiple_of(from_z % 2 * 256, 256), 256)
            block = kj_own[r * 2 * CORES + from_z // 2, rows, :]
            part = jnp.dot(a_refs[s][...], block, preferred_element_type=jnp.float32)
            total = part if total is None else total + part
        if r == 0:
            own[1].wait()
        t = total * x_refs[r][0].astype(jnp.float32)
        c = total * x_refs[r][1].astype(jnp.float32)
        trans = t if trans is None else trans + t
        cyc = c if cyc is None else cyc + c
    for e in range(tiles):
        place = jnp.where(e <= first, first - e, tiles + first - e)
        for which, full in ((0, trans), (1, cyc)):
            tile = full[e * TILE : (e + 1) * TILE, :]
            folded = (tile[:, :TILE] + tile[:, TILE:]).T
            res_ref[pl.ds(which * tiles + place, 1), :] = jnp.sum(folded, axis=0, keepdims=True)


def census(a_blocks, x_blocks, kj):
    a, x = a_blocks[0], x_blocks[0]
    left = [pltpu.with_memory_space_constraint(v, pltpu.HBM) for v in (a, x, kj)]
    return pl.pallas_call(
        census_kernel,
        out_shape=jax.ShapeDtypeStruct((8, TILE), jnp.float32),
        in_specs=[HBM] + [VMEM] * (ZS - 1) + [HBM] + [VMEM] * (XS - 1) + [HBM],
        out_specs=VMEM,
        scratch_shapes=[
            pltpu.VMEM(a.shape, a.dtype),
            pltpu.VMEM(x.shape, x.dtype),
            pltpu.VMEM(kj.shape, kj.dtype),
            pltpu.SemaphoreType.DMA((2,)),
            pltpu.SemaphoreType.DMA((ROWS,)),
        ],
        compiler_params=pltpu.CompilerParams(vmem_limit_bytes=18 * 2**20),
        name="census",
    )(left[0], *a_blocks[1:], left[1], *x_blocks[1:], left[2])


def per_device(out_weights, in_weights, tile_list, tile_count, owner):
    am, *leaving = prologue(out_weights, in_weights, tile_list, tile_count, owner)
    lines = to_lines(am)
    owned = [leaving[0]] + [along_row(leaving[e], e) for e in range(1, 4)]
    lines, *owned = lax.optimization_barrier((lines, *owned))
    kj = lax.all_gather(lines, "row", axis=0, tiled=False)
    mine, both = pack(owned)
    a = {0: mine}
    for s in range(1, ZS // 2):
        a[s] = along_z(a[s - 1], 1)
        a[ZS - s] = along_z(a[(ZS - s + 1) % ZS], -1)
    a[ZS // 2] = along_z(a[ZS // 2 - 1], 1)
    x = [both] + [along_x(both, r) for r in range(1, XS)]
    part = census([a[s] for s in range(ZS)], x, kj)
    sent = jnp.broadcast_to(part.reshape(1, 1, -1), (COLS, 1, part.size))
    total = lax.all_to_all(sent, "col", 0, 0, tiled=True).sum(axis=0)
    total = total.reshape(2, -1)
    return total[0], total[1]


def solution(mesh):
    in_specs = (P("row", "col"), P("row", "col"), P(), P(), P())
    return jax.shard_map(
        per_device, mesh=mesh, in_specs=in_specs, out_specs=(P("row"), P("row")), check_vma=False
    )
```

```python
import jax
import jax.numpy as jnp
from jax import lax
from jax.experimental import pallas as pl
from jax.experimental.pallas import tpu as pltpu
from jax.sharding import PartitionSpec as P

TILE = 128
XS, ZS, YS, CORES = 4, 8, 8, 2
ROWS, COLS = YS * CORES, XS * ZS
HBM = pl.BlockSpec(memory_space=pltpu.HBM)
VMEM = pl.BlockSpec(memory_space=pltpu.VMEM)
SMEM = pl.BlockSpec(memory_space=pltpu.SMEM)


def along_x(a, by):
    pairs = [(x * ZS + z, (x + by) % XS * ZS + z) for x in range(XS) for z in range(ZS)]
    return lax.ppermute(a, "col", pairs)


def along_z(a, by):
    pairs = [(x * ZS + z, x * ZS + (z + by) % ZS) for x in range(XS) for z in range(ZS)]
    return lax.ppermute(a, "col", pairs)


def along_row(a, by):
    return lax.ppermute(a, "row", [(i, (i + by) % ROWS) for i in range(ROWS)])


AWAY = (3, 2, 0, 1)


def to_lines(a):
    pairs = []
    for y in range(YS):
        for k in range(CORES):
            for x in range(XS):
                for z in range(ZS):
                    b = y // 2
                    away = AWAY[(x - b) % XS]
                    to_y = (y + away if y % 2 else y - away) % YS
                    src = (y * CORES + k) * COLS + x * ZS + z
                    dst = (to_y * CORES + k) * COLS + b * ZS + z
                    pairs.append((src, dst))
    return lax.ppermute(a, ("row", "col"), pairs)


def line_row(odd, x, b):
    ahead = lax.rem(x - b + XS, XS)
    away = jnp.where(ahead < 2, 3 - ahead, ahead - 2)
    return lax.rem(2 * b + odd * (1 + 2 * away) - away + YS, YS)


def prologue_kernel(out_ref, in_ref, list_ref, count_ref, owner_ref, am_ref, *e_refs):
    row, col = lax.axis_index("row"), lax.axis_index("col")
    tiles = out_ref.shape[0] // TILE
    slots, rows_total = list_ref.shape
    lane = lax.broadcasted_iota(jnp.int32, (1, rows_total), 1)
    live = lax.broadcasted_iota(jnp.int32, list_ref.shape, 0) < count_ref[...]

    def rows_with(b):
        hit = (list_ref[...] == b) & live
        return jnp.max(jnp.where(hit, 1.0, 0.0), axis=0, keepdims=True)

    has_col = [rows_with(col * 2 + q) for q in range(2)]
    has_row = [rows_with(row * tiles + t) for t in range(tiles)]

    def listed(vector, a):
        return jnp.max(jnp.where(lane == a, vector, 0.0), axis=1, keepdims=True)

    im_ref = e_refs[-1]
    for t in range(tiles):
        for q in range(2):
            rows, cols = pl.ds(t * TILE, TILE), pl.ds(q * TILE, TILE)
            keep = jnp.broadcast_to(listed(has_col[q], row * tiles + t), (TILE, TILE))
            am_ref[rows, cols] = out_ref[rows, cols] * keep.astype(out_ref.dtype)
            keep = jnp.broadcast_to(listed(has_row[t], col * 2 + q), (TILE, TILE))
            im_ref[rows, cols] = in_ref[rows, cols] * keep.astype(in_ref.dtype)
    for e in range(tiles):
        which = 0
        for t in range(1, tiles):
            offset = lax.rem(owner_ref[row * tiles + t] - row + ROWS, ROWS)
            which = jnp.where(offset == e, t, which)
        rows = pl.ds(pl.multiple_of(which * TILE, TILE), TILE)
        e_refs[e][0] = am_ref[rows, :]
        e_refs[e][1] = im_ref[rows, :]


def prologue(out_block, in_block, tile_list, tile_count, owner):
    rows, cols = out_block.shape
    tiles = rows // TILE
    dtype = out_block.dtype
    one = jax.ShapeDtypeStruct((2, TILE, cols), dtype)
    return pl.pallas_call(
        prologue_kernel,
        out_shape=[jax.ShapeDtypeStruct((rows, cols), dtype)] + [one] * tiles,
        in_specs=[VMEM, VMEM, VMEM, VMEM, SMEM],
        out_specs=[VMEM] * (1 + tiles),
        scratch_shapes=[pltpu.VMEM((rows, cols), dtype)],
        name="prologue",
    )(out_block, in_block, tile_list.T, tile_count[None, :], owner)


def pack_kernel(*refs):
    mine_ref, both_ref = refs[-2:]
    for e, ref in enumerate(refs[:-2]):
        rows = pl.ds(e * TILE, TILE)
        mine_ref[rows, :] = ref[0]
        both_ref[0, rows, :] = ref[0]
        both_ref[1, rows, :] = ref[1]


def pack(owned):
    _, tile, cols = owned[0].shape
    rows, dtype = len(owned) * tile, owned[0].dtype
    return pl.pallas_call(
        pack_kernel,
        out_shape=[
            jax.ShapeDtypeStruct((rows, cols), dtype),
            jax.ShapeDtypeStruct((2, rows, cols), dtype),
        ],
        in_specs=[VMEM] * len(owned),
        out_specs=[VMEM] * 2,
        name="pack",
    )(*owned)


EARLY = (1, 7, 2, 6, 3, 5, 0)
LAST = ZS // 2


def block_of(kj_ref, r, s):
    col = lax.axis_index("col")
    from_x = lax.rem(col // ZS + XS - r, XS)
    from_z = lax.rem(col % ZS + ZS - s, ZS)
    shard = line_row(from_z // 4, from_x, col // ZS) * CORES + from_z % 4 // 2
    rows = pl.ds(pl.multiple_of(from_z % 2 * 256, 256), 256)
    return kj_ref[shard, rows, :]


def products_kernel(*refs):
    a_refs, own_ref = refs[: len(EARLY) - 1], refs[len(EARLY) - 1]
    kj_ref, acc_ref, a_own, sem = refs[len(EARLY) :]
    own = pltpu.make_async_copy(own_ref, a_own, sem)
    own.start()
    for r in range(XS):
        total = None
        for n, s in enumerate(EARLY):
            if s == 0 and r == 0:
                own.wait()
            rows = a_own[...] if s == 0 else a_refs[n][...]
            part = jnp.dot(rows, block_of(kj_ref, r, s), preferred_element_type=jnp.float32)
            total = part if total is None else total + part
        acc_ref[r] = total


def products(a, kj):
    own = pltpu.with_memory_space_constraint(a[0], pltpu.HBM)
    rows, cols = own.shape
    return pl.pallas_call(
        products_kernel,
        out_shape=jax.ShapeDtypeStruct((XS, rows, cols), jnp.float32),
        in_specs=[VMEM] * (len(EARLY) - 1) + [HBM, VMEM],
        out_specs=VMEM,
        scratch_shapes=[pltpu.VMEM(own.shape, own.dtype), pltpu.SemaphoreType.DMA],
        compiler_params=pltpu.CompilerParams(vmem_limit_bytes=12 * 2**20),
        name="products",
    )(*[a[s] for s in EARLY[:-1]], own, kj)


def census_kernel(acc_ref, a_ref, kj_ref, *refs):
    x_refs, own_ref = refs[: XS - 1], refs[XS - 1]
    res_ref, x_own, sem = refs[XS:]
    own = pltpu.make_async_copy(own_ref, x_own, sem)
    own.start()
    row = lax.axis_index("row")
    tiles = 4
    first = jnp.minimum(row, tiles - 1)
    trans = cyc = None
    for r in (1, 2, 3, 0):
        block = block_of(kj_ref, r, LAST)
        total = acc_ref[r] + jnp.dot(a_ref[...], block, preferred_element_type=jnp.float32)
        if r == 0:
            own.wait()
        x_ref = x_refs[r - 1] if r else x_own
        t = total * x_ref[0].astype(jnp.float32)
        c = total * x_ref[1].astype(jnp.float32)
        trans = t if trans is None else trans + t
        cyc = c if cyc is None else cyc + c
    for e in range(tiles):
        place = jnp.where(e <= first, first - e, tiles + first - e)
        for which, full in ((0, trans), (1, cyc)):
            tile = full[e * TILE : (e + 1) * TILE, :]
            folded = (tile[:, :TILE] + tile[:, TILE:]).T
            res_ref[pl.ds(which * tiles + place, 1), :] = jnp.sum(folded, axis=0, keepdims=True)


def census(acc, last, kj, x):
    own = pltpu.with_memory_space_constraint(x[0], pltpu.HBM)
    return pl.pallas_call(
        census_kernel,
        out_shape=jax.ShapeDtypeStruct((8, TILE), jnp.float32),
        in_specs=[VMEM] * (3 + XS - 1) + [HBM],
        out_specs=VMEM,
        scratch_shapes=[pltpu.VMEM(own.shape, own.dtype), pltpu.SemaphoreType.DMA],
        compiler_params=pltpu.CompilerParams(vmem_limit_bytes=12 * 2**20),
        name="census",
    )(acc, last, kj, *x[1:], own)


def per_device(out_weights, in_weights, tile_list, tile_count, owner):
    am, *leaving = prologue(out_weights, in_weights, tile_list, tile_count, owner)
    lines = to_lines(am)
    owned = [leaving[0]] + [along_row(leaving[e], e) for e in range(1, 4)]
    lines, *owned = lax.optimization_barrier((lines, *owned))
    kj = lax.all_gather(lines, "row", axis=0, tiled=False)
    mine, both = pack(owned)
    a = {0: mine}
    for s in range(1, ZS // 2):
        a[s] = along_z(a[s - 1], 1)
        a[ZS - s] = along_z(a[(ZS - s + 1) % ZS], -1)
    a[ZS // 2] = along_z(a[ZS // 2 - 1], 1)
    x = [both] + [along_x(both, r) for r in range(1, XS)]
    part = census(products(a, kj), a[LAST], kj, x)
    sent = jnp.broadcast_to(part.reshape(1, 1, -1), (COLS, 1, part.size))
    total = lax.all_to_all(sent, "col", 0, 0, tiled=True).sum(axis=0)
    total = total.reshape(2, -1)
    return total[0], total[1]


def solution(mesh):
    in_specs = (P("row", "col"), P("row", "col"), P(), P(), P())
    return jax.shard_map(
        per_device, mesh=mesh, in_specs=in_specs, out_specs=(P("row"), P("row")), check_vma=False
    )
```

```python
import jax
import jax.numpy as jnp
from jax import lax
from jax.experimental import pallas as pl
from jax.experimental.pallas import tpu as pltpu
from jax.sharding import PartitionSpec as P

TILE = 128
XS, ZS, YS, CORES = 4, 8, 8, 2
ROWS, COLS = YS * CORES, XS * ZS
HBM = pl.BlockSpec(memory_space=pltpu.HBM)
VMEM = pl.BlockSpec(memory_space=pltpu.VMEM)
SMEM = pl.BlockSpec(memory_space=pltpu.SMEM)


def along_x(a, by):
    pairs = [(x * ZS + z, (x + by) % XS * ZS + z) for x in range(XS) for z in range(ZS)]
    return lax.ppermute(a, "col", pairs)


def along_z(a, by):
    pairs = [(x * ZS + z, x * ZS + (z + by) % ZS) for x in range(XS) for z in range(ZS)]
    return lax.ppermute(a, "col", pairs)


def along_row(a, by):
    return lax.ppermute(a, "row", [(i, (i + by) % ROWS) for i in range(ROWS)])


AWAY = (3, 2, 0, 1)


def to_lines(a):
    pairs = []
    for y in range(YS):
        for k in range(CORES):
            for x in range(XS):
                for z in range(ZS):
                    b = y // 2
                    away = AWAY[(x - b) % XS]
                    to_y = (y + away if y % 2 else y - away) % YS
                    src = (y * CORES + k) * COLS + x * ZS + z
                    dst = (to_y * CORES + k) * COLS + b * ZS + z
                    pairs.append((src, dst))
    return lax.ppermute(a, ("row", "col"), pairs)


def kept_on_chip(arrays):
    return [pltpu.with_memory_space_constraint(a, pltpu.VMEM) for a in arrays]


def line_row(odd, x, b):
    ahead = lax.rem(x - b + XS, XS)
    away = jnp.where(ahead < 2, 3 - ahead, ahead - 2)
    return lax.rem(2 * b + odd * (1 + 2 * away) - away + YS, YS)


def prologue_kernel(out_ref, in_ref, list_ref, count_ref, owner_ref, am_ref, *e_refs):
    row, col = lax.axis_index("row"), lax.axis_index("col")
    tiles = out_ref.shape[0] // TILE
    slots, rows_total = list_ref.shape
    lane = lax.broadcasted_iota(jnp.int32, (1, rows_total), 1)
    live = lax.broadcasted_iota(jnp.int32, list_ref.shape, 0) < count_ref[...]

    def rows_with(b):
        hit = (list_ref[...] == b) & live
        return jnp.max(jnp.where(hit, 1.0, 0.0), axis=0, keepdims=True)

    has_col = [rows_with(col * 2 + q) for q in range(2)]
    has_row = [rows_with(row * tiles + t) for t in range(tiles)]

    def listed(vector, a):
        return jnp.max(jnp.where(lane == a, vector, 0.0), axis=1, keepdims=True)

    im_ref = e_refs[-1]
    for t in range(tiles):
        for q in range(2):
            rows, cols = pl.ds(t * TILE, TILE), pl.ds(q * TILE, TILE)
            keep = jnp.broadcast_to(listed(has_col[q], row * tiles + t), (TILE, TILE))
            am_ref[rows, cols] = out_ref[rows, cols] * keep.astype(out_ref.dtype)
            keep = jnp.broadcast_to(listed(has_row[t], col * 2 + q), (TILE, TILE))
            im_ref[rows, cols] = in_ref[rows, cols] * keep.astype(in_ref.dtype)
    for e in range(tiles):
        which = 0
        for t in range(1, tiles):
            offset = lax.rem(owner_ref[row * tiles + t] - row + ROWS, ROWS)
            which = jnp.where(offset == e, t, which)
        rows = pl.ds(pl.multiple_of(which * TILE, TILE), TILE)
        e_refs[e][0] = am_ref[rows, :]
        e_refs[e][1] = im_ref[rows, :]


def prologue(out_block, in_block, tile_list, tile_count, owner):
    rows, cols = out_block.shape
    tiles = rows // TILE
    dtype = out_block.dtype
    one = jax.ShapeDtypeStruct((2, TILE, cols), dtype)
    return pl.pallas_call(
        prologue_kernel,
        out_shape=[jax.ShapeDtypeStruct((rows, cols), dtype)] + [one] * tiles,
        in_specs=[VMEM, VMEM, VMEM, VMEM, SMEM],
        out_specs=[VMEM] * (1 + tiles),
        scratch_shapes=[pltpu.VMEM((rows, cols), dtype)],
        name="prologue",
    )(out_block, in_block, tile_list.T, tile_count[None, :], owner)


def pack_kernel(*refs):
    mine_ref, both_ref = refs[-2:]
    for e, ref in enumerate(refs[:-2]):
        rows = pl.ds(e * TILE, TILE)
        mine_ref[rows, :] = ref[0]
        both_ref[0, rows, :] = ref[0]
        both_ref[1, rows, :] = ref[1]


def pack(owned):
    _, tile, cols = owned[0].shape
    rows, dtype = len(owned) * tile, owned[0].dtype
    return pl.pallas_call(
        pack_kernel,
        out_shape=[
            jax.ShapeDtypeStruct((rows, cols), dtype),
            jax.ShapeDtypeStruct((2, rows, cols), dtype),
        ],
        in_specs=[VMEM] * len(owned),
        out_specs=[VMEM] * 2,
        name="pack",
    )(*owned)


EARLY = (1, 7, 2, 6, 3, 5, 0)
LAST = ZS // 2


def block_of(kj_ref, r, s):
    col = lax.axis_index("col")
    from_x = lax.rem(col // ZS + XS - r, XS)
    from_z = lax.rem(col % ZS + ZS - s, ZS)
    shard = line_row(from_z // 4, from_x, col // ZS) * CORES + from_z % 4 // 2
    rows = pl.ds(pl.multiple_of(from_z % 2 * 256, 256), 256)
    return kj_ref[shard, rows, :]


def products_kernel(*refs):
    a_refs, own_ref = refs[: len(EARLY) - 1], refs[len(EARLY) - 1]
    kj_ref, acc_ref, last_ref, a_own, sem = refs[len(EARLY) :]
    own = pltpu.make_async_copy(own_ref, a_own, sem)
    own.start()
    for r in range(XS):
        total = None
        for a_ref, s in zip(a_refs, EARLY):
            part = jnp.dot(a_ref[...], block_of(kj_ref, r, s), preferred_element_type=jnp.float32)
            total = part if total is None else total + part
        if r == XS - 1:
            own.wait()
            block = block_of(kj_ref, r, 0)
            total += jnp.dot(a_own[...], block, preferred_element_type=jnp.float32)
        acc_ref[r] = total
        last_ref[r] = block_of(kj_ref, r, LAST)
    for r in range(XS - 1):
        block = block_of(kj_ref, r, 0)
        acc_ref[r] += jnp.dot(a_own[...], block, preferred_element_type=jnp.float32)


def products(a, kj):
    own = pltpu.with_memory_space_constraint(a[0], pltpu.HBM)
    rows, cols = own.shape
    return pl.pallas_call(
        products_kernel,
        out_shape=[
            jax.ShapeDtypeStruct((XS, rows, cols), jnp.float32),
            jax.ShapeDtypeStruct((XS, cols, cols), kj.dtype),
        ],
        in_specs=[VMEM] * (len(EARLY) - 1) + [HBM, VMEM],
        out_specs=[VMEM] * 2,
        scratch_shapes=[pltpu.VMEM(own.shape, own.dtype), pltpu.SemaphoreType.DMA],
        compiler_params=pltpu.CompilerParams(vmem_limit_bytes=12 * 2**20),
        name="products",
    )(*[a[s] for s in EARLY[:-1]], own, kj)


def census_kernel(acc_ref, last_ref, a_ref, *refs):
    x_refs, res_ref = refs[:XS], refs[XS]
    row = lax.axis_index("row")
    tiles = 4
    first = jnp.minimum(row, tiles - 1)
    trans = cyc = None
    for r in range(XS):
        part = jnp.dot(a_ref[...], last_ref[r], preferred_element_type=jnp.float32)
        total = acc_ref[r] + part
        t = total * x_refs[r][0].astype(jnp.float32)
        c = total * x_refs[r][1].astype(jnp.float32)
        trans = t if trans is None else trans + t
        cyc = c if cyc is None else cyc + c
    for e in range(tiles):
        place = jnp.where(e <= first, first - e, tiles + first - e)
        for which, full in ((0, trans), (1, cyc)):
            tile = full[e * TILE : (e + 1) * TILE, :]
            folded = (tile[:, :TILE] + tile[:, TILE:]).T
            res_ref[pl.ds(which * tiles + place, 1), :] = jnp.sum(folded, axis=0, keepdims=True)


def census(acc, last, a, x):
    return pl.pallas_call(
        census_kernel,
        out_shape=jax.ShapeDtypeStruct((8, TILE), jnp.float32),
        in_specs=[VMEM] * (3 + XS),
        out_specs=VMEM,
        compiler_params=pltpu.CompilerParams(vmem_limit_bytes=12 * 2**20),
        name="census",
    )(acc, last, a, *x)


def per_device(out_weights, in_weights, tile_list, tile_count, owner):
    am, *leaving = prologue(out_weights, in_weights, tile_list, tile_count, owner)
    lines = to_lines(am)
    owned = [leaving[0]] + [along_row(leaving[e], e) for e in range(1, 4)]
    lines, *owned = lax.optimization_barrier((lines, *owned))
    kj = lax.all_gather(lines, "row", axis=0, tiled=False)
    mine, both = pack([owned[0], *kept_on_chip(owned[1:])])
    a = {0: mine}
    for s in range(1, ZS // 2):
        a[s] = along_z(a[s - 1], 1)
        a[ZS - s] = along_z(a[(ZS - s + 1) % ZS], -1)
    a[ZS // 2] = along_z(a[ZS // 2 - 1], 1)
    x = [both] + [along_x(both, r) for r in range(1, XS)]
    part = census(*products(a, kj), a[LAST], x)
    sent = jnp.broadcast_to(part.reshape(1, 1, -1), (COLS, 1, part.size))
    total = lax.all_to_all(sent, "col", 0, 0, tiled=True).sum(axis=0)
    total = total.reshape(2, -1)
    return total[0], total[1]


def solution(mesh):
    in_specs = (P("row", "col"), P("row", "col"), P(), P(), P())
    return jax.shard_map(
        per_device, mesh=mesh, in_specs=in_specs, out_specs=(P("row"), P("row")), check_vma=False
    )
```

```python
import jax
import jax.numpy as jnp
from jax import lax
from jax.experimental import pallas as pl
from jax.experimental.pallas import tpu as pltpu
from jax.sharding import PartitionSpec as P

TILE = 128
XS, ZS, YS, CORES = 4, 8, 8, 2
ROWS, COLS = YS * CORES, XS * ZS
HBM = pl.BlockSpec(memory_space=pltpu.HBM)
VMEM = pl.BlockSpec(memory_space=pltpu.VMEM)
SMEM = pl.BlockSpec(memory_space=pltpu.SMEM)


def along_x(a, by):
    pairs = [(x * ZS + z, (x + by) % XS * ZS + z) for x in range(XS) for z in range(ZS)]
    return lax.ppermute(a, "col", pairs)


def along_z(a, by):
    pairs = [(x * ZS + z, x * ZS + (z + by) % ZS) for x in range(XS) for z in range(ZS)]
    return lax.ppermute(a, "col", pairs)


def along_row(a, by):
    return lax.ppermute(a, "row", [(i, (i + by) % ROWS) for i in range(ROWS)])


AWAY = (3, 2, 0, 1)


def to_lines(a):
    pairs = []
    for y in range(YS):
        for k in range(CORES):
            for x in range(XS):
                for z in range(ZS):
                    b = y // 2
                    away = AWAY[(x - b) % XS]
                    to_y = (y + away if y % 2 else y - away) % YS
                    src = (y * CORES + k) * COLS + x * ZS + z
                    dst = (to_y * CORES + k) * COLS + b * ZS + z
                    pairs.append((src, dst))
    return lax.ppermute(a, ("row", "col"), pairs)


def kept_on_chip(arrays):
    return [pltpu.with_memory_space_constraint(a, pltpu.VMEM) for a in arrays]


def line_row(odd, x, b):
    ahead = lax.rem(x - b + XS, XS)
    away = jnp.where(ahead < 2, 3 - ahead, ahead - 2)
    return lax.rem(2 * b + odd * (1 + 2 * away) - away + YS, YS)


def prologue_kernel(out_ref, in_ref, list_ref, count_ref, owner_ref, am_ref, *e_refs):
    row, col = lax.axis_index("row"), lax.axis_index("col")
    tiles = out_ref.shape[0] // TILE
    slots, rows_total = list_ref.shape
    lane = lax.broadcasted_iota(jnp.int32, (1, rows_total), 1)
    live = lax.broadcasted_iota(jnp.int32, list_ref.shape, 0) < count_ref[...]

    def rows_with(b):
        hit = (list_ref[...] == b) & live
        return jnp.max(jnp.where(hit, 1.0, 0.0), axis=0, keepdims=True)

    has_col = [rows_with(col * 2 + q) for q in range(2)]
    has_row = [rows_with(row * tiles + t) for t in range(tiles)]

    def listed(vector, a):
        return jnp.max(jnp.where(lane == a, vector, 0.0), axis=1, keepdims=True)

    im_ref = e_refs[-1]
    for t in range(tiles):
        for q in range(2):
            rows, cols = pl.ds(t * TILE, TILE), pl.ds(q * TILE, TILE)
            keep = jnp.broadcast_to(listed(has_col[q], row * tiles + t), (TILE, TILE))
            am_ref[rows, cols] = out_ref[rows, cols] * keep.astype(out_ref.dtype)
            keep = jnp.broadcast_to(listed(has_row[t], col * 2 + q), (TILE, TILE))
            im_ref[rows, cols] = in_ref[rows, cols] * keep.astype(in_ref.dtype)
    for e in range(tiles):
        which = 0
        for t in range(1, tiles):
            offset = lax.rem(owner_ref[row * tiles + t] - row + ROWS, ROWS)
            which = jnp.where(offset == e, t, which)
        rows = pl.ds(pl.multiple_of(which * TILE, TILE), TILE)
        e_refs[e][0] = am_ref[rows, :]
        e_refs[e][1] = im_ref[rows, :]


def prologue(out_block, in_block, tile_list, tile_count, owner):
    rows, cols = out_block.shape
    tiles = rows // TILE
    dtype = out_block.dtype
    one = jax.ShapeDtypeStruct((2, TILE, cols), dtype)
    return pl.pallas_call(
        prologue_kernel,
        out_shape=[jax.ShapeDtypeStruct((rows, cols), dtype)] + [one] * tiles,
        in_specs=[VMEM, VMEM, VMEM, VMEM, SMEM],
        out_specs=[VMEM] * (1 + tiles),
        scratch_shapes=[pltpu.VMEM((rows, cols), dtype)],
        name="prologue",
    )(out_block, in_block, tile_list.T, tile_count[None, :], owner)


def pack_kernel(*refs):
    mine_ref, both_ref = refs[-2:]
    for e, ref in enumerate(refs[:-2]):
        rows = pl.ds(e * TILE, TILE)
        mine_ref[rows, :] = ref[0]
        both_ref[0, rows, :] = ref[0]
        both_ref[1, rows, :] = ref[1]


def pack(owned):
    _, tile, cols = owned[0].shape
    rows, dtype = len(owned) * tile, owned[0].dtype
    return pl.pallas_call(
        pack_kernel,
        out_shape=[
            jax.ShapeDtypeStruct((rows, cols), dtype),
            jax.ShapeDtypeStruct((2, rows, cols), dtype),
        ],
        in_specs=[VMEM] * len(owned),
        out_specs=[VMEM] * 2,
        name="pack",
    )(*owned)


EARLY = (1, 7, 2, 6, 3, 5, 0)
LAST = ZS // 2


def block_of(kj_ref, r, s):
    col = lax.axis_index("col")
    from_x = lax.rem(col // ZS + XS - r, XS)
    from_z = lax.rem(col % ZS + ZS - s, ZS)
    shard = line_row(from_z // 4, from_x, col // ZS) * CORES + from_z % 4 // 2
    rows = pl.ds(pl.multiple_of(from_z % 2 * 256, 256), 256)
    return kj_ref[shard, rows, :]


def products_kernel(*refs):
    a_refs, own_ref = refs[: len(EARLY) - 1], refs[len(EARLY) - 1]
    kj_ref, acc_ref, last_ref, a_own, sem = refs[len(EARLY) :]
    own = pltpu.make_async_copy(own_ref, a_own, sem)
    own.start()
    for r in range(XS):
        total = None
        for a_ref, s in zip(a_refs, EARLY):
            part = jnp.dot(a_ref[...], block_of(kj_ref, r, s), preferred_element_type=jnp.float32)
            total = part if total is None else total + part
        if r == XS - 1:
            own.wait()
            block = block_of(kj_ref, r, 0)
            total += jnp.dot(a_own[...], block, preferred_element_type=jnp.float32)
        acc_ref[r] = total
        last_ref[r] = block_of(kj_ref, r, LAST)
    for r in range(XS - 1):
        block = block_of(kj_ref, r, 0)
        acc_ref[r] += jnp.dot(a_own[...], block, preferred_element_type=jnp.float32)


def products(a, kj):
    own = pltpu.with_memory_space_constraint(a[0], pltpu.HBM)
    rows, cols = own.shape
    return pl.pallas_call(
        products_kernel,
        out_shape=[
            jax.ShapeDtypeStruct((XS, rows, cols), jnp.float32),
            jax.ShapeDtypeStruct((XS, cols, cols), kj.dtype),
        ],
        in_specs=[VMEM] * (len(EARLY) - 1) + [HBM, VMEM],
        out_specs=[VMEM] * 2,
        scratch_shapes=[pltpu.VMEM(own.shape, own.dtype), pltpu.SemaphoreType.DMA],
        compiler_params=pltpu.CompilerParams(vmem_limit_bytes=12 * 2**20),
        name="products",
    )(*[a[s] for s in EARLY[:-1]], own, kj)


def census_kernel(acc_ref, last_ref, a_ref, *refs):
    x_refs, res_ref = refs[:XS], refs[XS]
    row = lax.axis_index("row")
    tiles = 4
    first = jnp.minimum(row, tiles - 1)
    trans = cyc = None
    for r in range(XS):
        part = jnp.dot(a_ref[...], last_ref[r], preferred_element_type=jnp.float32)
        total = acc_ref[r] + part
        t = total * x_refs[r][0].astype(jnp.float32)
        c = total * x_refs[r][1].astype(jnp.float32)
        trans = t if trans is None else trans + t
        cyc = c if cyc is None else cyc + c
    for e in range(tiles):
        place = jnp.where(e <= first, first - e, tiles + first - e)
        for which, full in ((0, trans), (1, cyc)):
            tile = full[e * TILE : (e + 1) * TILE, :]
            folded = (tile[:, :TILE] + tile[:, TILE:]).T
            res_ref[pl.ds(which * tiles + place, 1), :] = jnp.sum(folded, axis=0, keepdims=True)


def census(acc, last, a, x):
    return pl.pallas_call(
        census_kernel,
        out_shape=jax.ShapeDtypeStruct((8, TILE), jnp.float32),
        in_specs=[VMEM] * (3 + XS),
        out_specs=VMEM,
        compiler_params=pltpu.CompilerParams(vmem_limit_bytes=12 * 2**20),
        name="census",
    )(acc, last, a, *x)


def per_device(out_weights, in_weights, tile_list, tile_count, owner):
    am, *leaving = prologue(out_weights, in_weights, tile_list, tile_count, owner)
    lines = to_lines(am)
    owned = [leaving[0]] + [along_row(leaving[e], e) for e in range(1, 4)]
    lines, *owned[2:] = lax.optimization_barrier((lines, *owned[2:]))
    kj = lax.all_gather(lines, "row", axis=0, tiled=False)
    mine, both = pack([owned[0], *kept_on_chip(owned[1:])])
    a = {0: mine}
    for s in range(1, ZS // 2):
        a[s] = along_z(a[s - 1], 1)
        a[ZS - s] = along_z(a[(ZS - s + 1) % ZS], -1)
    a[ZS // 2] = along_z(a[ZS // 2 - 1], 1)
    x = [both] + [along_x(both, r) for r in range(1, XS)]
    part = census(*products(a, kj), a[LAST], x)
    sent = jnp.broadcast_to(part.reshape(1, 1, -1), (COLS, 1, part.size))
    total = lax.all_to_all(sent, "col", 0, 0, tiled=True).sum(axis=0)
    total = total.reshape(2, -1)
    return total[0], total[1]


def solution(mesh):
    in_specs = (P("row", "col"), P("row", "col"), P(), P(), P())
    return jax.shard_map(
        per_device, mesh=mesh, in_specs=in_specs, out_specs=(P("row"), P("row")), check_vma=False
    )
```

```python
import jax
import jax.numpy as jnp
from jax import lax
from jax.experimental import pallas as pl
from jax.experimental.pallas import tpu as pltpu
from jax.sharding import PartitionSpec as P

TILE = 128
XS, ZS, YS, CORES = 4, 8, 8, 2
ROWS, COLS = YS * CORES, XS * ZS
HBM = pl.BlockSpec(memory_space=pltpu.HBM)
VMEM = pl.BlockSpec(memory_space=pltpu.VMEM)
SMEM = pl.BlockSpec(memory_space=pltpu.SMEM)


def along_x(a, by):
    pairs = [(x * ZS + z, (x + by) % XS * ZS + z) for x in range(XS) for z in range(ZS)]
    return lax.ppermute(a, "col", pairs)


def along_z(a, by):
    pairs = [(x * ZS + z, x * ZS + (z + by) % ZS) for x in range(XS) for z in range(ZS)]
    return lax.ppermute(a, "col", pairs)


def along_row(a, by):
    return lax.ppermute(a, "row", [(i, (i + by) % ROWS) for i in range(ROWS)])


AWAY = (3, 2, 0, 1)


def to_lines(a):
    pairs = []
    for y in range(YS):
        for k in range(CORES):
            for x in range(XS):
                for z in range(ZS):
                    b = y // 2
                    away = AWAY[(x - b) % XS]
                    to_y = (y + away if y % 2 else y - away) % YS
                    src = (y * CORES + k) * COLS + x * ZS + z
                    dst = (to_y * CORES + k) * COLS + b * ZS + z
                    pairs.append((src, dst))
    return lax.ppermute(a, ("row", "col"), pairs)


def kept_on_chip(arrays):
    return [pltpu.with_memory_space_constraint(a, pltpu.VMEM) for a in arrays]


def line_row(odd, x, b):
    ahead = lax.rem(x - b + XS, XS)
    away = jnp.where(ahead < 2, 3 - ahead, ahead - 2)
    return lax.rem(2 * b + odd * (1 + 2 * away) - away + YS, YS)


def prologue_kernel(out_ref, in_ref, list_ref, count_ref, owner_ref, am_ref, *e_refs):
    row, col = lax.axis_index("row"), lax.axis_index("col")
    tiles = out_ref.shape[0] // TILE
    slots, rows_total = list_ref.shape
    lane = lax.broadcasted_iota(jnp.int32, (1, rows_total), 1)
    live = lax.broadcasted_iota(jnp.int32, list_ref.shape, 0) < count_ref[...]

    def rows_with(b):
        hit = (list_ref[...] == b) & live
        return jnp.max(jnp.where(hit, 1.0, 0.0), axis=0, keepdims=True)

    has_col = [rows_with(col * 2 + q) for q in range(2)]
    has_row = [rows_with(row * tiles + t) for t in range(tiles)]

    def listed(vector, a):
        return jnp.max(jnp.where(lane == a, vector, 0.0), axis=1, keepdims=True)

    im_ref = e_refs[-1]
    for t in range(tiles):
        for q in range(2):
            rows, cols = pl.ds(t * TILE, TILE), pl.ds(q * TILE, TILE)
            keep = jnp.broadcast_to(listed(has_col[q], row * tiles + t), (TILE, TILE))
            am_ref[rows, cols] = out_ref[rows, cols] * keep.astype(out_ref.dtype)
            keep = jnp.broadcast_to(listed(has_row[t], col * 2 + q), (TILE, TILE))
            im_ref[rows, cols] = in_ref[rows, cols] * keep.astype(in_ref.dtype)
    for e in range(tiles):
        which = 0
        for t in range(1, tiles):
            offset = lax.rem(owner_ref[row * tiles + t] - row + ROWS, ROWS)
            which = jnp.where(offset == e, t, which)
        rows = pl.ds(pl.multiple_of(which * TILE, TILE), TILE)
        e_refs[e][0] = am_ref[rows, :]
        e_refs[e][1] = im_ref[rows, :]


def prologue(out_block, in_block, tile_list, tile_count, owner):
    rows, cols = out_block.shape
    tiles = rows // TILE
    dtype = out_block.dtype
    one = jax.ShapeDtypeStruct((2, TILE, cols), dtype)
    return pl.pallas_call(
        prologue_kernel,
        out_shape=[jax.ShapeDtypeStruct((rows, cols), dtype)] + [one] * tiles,
        in_specs=[VMEM, VMEM, VMEM, VMEM, SMEM],
        out_specs=[VMEM] * (1 + tiles),
        scratch_shapes=[pltpu.VMEM((rows, cols), dtype)],
        name="prologue",
    )(out_block, in_block, tile_list.T, tile_count[None, :], owner)


def pack_kernel(*refs):
    mine_ref, both_ref = refs[-2:]
    for e, ref in enumerate(refs[:-2]):
        rows = pl.ds(e * TILE, TILE)
        mine_ref[rows, :] = ref[0]
        both_ref[0, rows, :] = ref[0]
        both_ref[1, rows, :] = ref[1]


def pack(owned):
    _, tile, cols = owned[0].shape
    rows, dtype = len(owned) * tile, owned[0].dtype
    return pl.pallas_call(
        pack_kernel,
        out_shape=[
            jax.ShapeDtypeStruct((rows, cols), dtype),
            jax.ShapeDtypeStruct((2, rows, cols), dtype),
        ],
        in_specs=[VMEM] * len(owned),
        out_specs=[VMEM] * 2,
        name="pack",
    )(*owned)


EARLY = (1, 7, 2, 6, 3, 5, 0)
LAST = ZS // 2


def block_of(kj_ref, r, s):
    col = lax.axis_index("col")
    from_x = lax.rem(col // ZS + XS - r, XS)
    from_z = lax.rem(col % ZS + ZS - s, ZS)
    shard = line_row(from_z // 4, from_x, col // ZS) * CORES + from_z % 4 // 2
    rows = pl.ds(pl.multiple_of(from_z % 2 * 256, 256), 256)
    return kj_ref[shard, rows, :]


def products_kernel(*refs):
    a_refs, own_ref = refs[: len(EARLY) - 1], refs[len(EARLY) - 1]
    kj_ref, acc_ref, last_ref, a_own, sem = refs[len(EARLY) :]
    own = pltpu.make_async_copy(own_ref, a_own, sem)
    own.start()
    for r in range(XS):
        total = None
        for a_ref, s in zip(a_refs, EARLY):
            part = jnp.dot(a_ref[...], block_of(kj_ref, r, s), preferred_element_type=jnp.float32)
            total = part if total is None else total + part
        if r == XS - 1:
            own.wait()
            block = block_of(kj_ref, r, 0)
            total += jnp.dot(a_own[...], block, preferred_element_type=jnp.float32)
        acc_ref[r] = total
        last_ref[r] = block_of(kj_ref, r, LAST)
    for r in range(XS - 1):
        block = block_of(kj_ref, r, 0)
        acc_ref[r] += jnp.dot(a_own[...], block, preferred_element_type=jnp.float32)


def products(a, kj):
    own = pltpu.with_memory_space_constraint(a[0], pltpu.HBM)
    rows, cols = own.shape
    return pl.pallas_call(
        products_kernel,
        out_shape=[
            jax.ShapeDtypeStruct((XS, rows, cols), jnp.float32),
            jax.ShapeDtypeStruct((XS, cols, cols), kj.dtype),
        ],
        in_specs=[VMEM] * (len(EARLY) - 1) + [HBM, VMEM],
        out_specs=[VMEM] * 2,
        scratch_shapes=[pltpu.VMEM(own.shape, own.dtype), pltpu.SemaphoreType.DMA],
        compiler_params=pltpu.CompilerParams(vmem_limit_bytes=12 * 2**20),
        name="products",
    )(*[a[s] for s in EARLY[:-1]], own, kj)


def census_kernel(acc_ref, last_ref, a_ref, *refs):
    x_refs, res_ref = refs[:XS], refs[XS]
    row = lax.axis_index("row")
    tiles = 4
    first = jnp.minimum(row, tiles - 1)
    trans = cyc = None
    for r in range(XS):
        part = jnp.dot(a_ref[...], last_ref[r], preferred_element_type=jnp.float32)
        total = acc_ref[r] + part
        t = total * x_refs[r][0].astype(jnp.float32)
        c = total * x_refs[r][1].astype(jnp.float32)
        trans = t if trans is None else trans + t
        cyc = c if cyc is None else cyc + c
    for e in range(tiles):
        place = jnp.where(e <= first, first - e, tiles + first - e)
        for which, full in ((0, trans), (1, cyc)):
            tile = full[e * TILE : (e + 1) * TILE, :]
            folded = (tile[:, :TILE] + tile[:, TILE:]).T
            res_ref[pl.ds(which * tiles + place, 1), :] = jnp.sum(folded, axis=0, keepdims=True)


def census(acc, last, a, x):
    return pl.pallas_call(
        census_kernel,
        out_shape=jax.ShapeDtypeStruct((8, TILE), jnp.float32),
        in_specs=[VMEM] * (3 + XS),
        out_specs=VMEM,
        compiler_params=pltpu.CompilerParams(vmem_limit_bytes=12 * 2**20),
        name="census",
    )(acc, last, a, *x)


def per_device(out_weights, in_weights, tile_list, tile_count, owner):
    am, *leaving = prologue(out_weights, in_weights, tile_list, tile_count, owner)
    lines = to_lines(am)
    owned = [leaving[0]] + [along_row(leaving[e], e) for e in range(1, 4)]
    lines, *owned = lax.optimization_barrier((lines, *owned))
    kj = lax.all_gather(lines, "row", axis=0, tiled=False)
    mine, both = pack([owned[0], *kept_on_chip(owned[1:])])
    a = {0: mine}
    for s in range(1, ZS // 2):
        a[s] = along_z(a[s - 1], 1)
        a[ZS - s] = along_z(a[(ZS - s + 1) % ZS], -1)
    a[ZS // 2] = along_z(a[ZS // 2 - 1], 1)
    x = [both] + [along_x(both, r) for r in range(1, XS)]
    part = census(*products(a, kj), a[LAST], x)
    sent = jnp.broadcast_to(part.reshape(1, 1, -1), (COLS, 1, part.size))
    shares = lax.all_to_all(sent, "col", 0, 0, tiled=True)[:, 0]
    nodes = part.size // 2
    return shares[:, :nodes].sum(axis=0), shares[:, nodes:].sum(axis=0)


def solution(mesh):
    in_specs = (P("row", "col"), P("row", "col"), P(), P(), P())
    return jax.shard_map(
        per_device, mesh=mesh, in_specs=in_specs, out_specs=(P("row"), P("row")), check_vma=False
    )
```
